256 devices in a mesh: gx: 4 (over x), gy: 8 (over z_hi, core), gz: 8 (over y, z_lo).
Axes of the slice: x: 4, y: 4, z: 8 (z_hi: 4, z_lo: 2; z = z_hi * 2 + z_lo), core: 2. Of those that a mesh axis runs over, the one named last changes fastest.
Arguments:
- state: float32 [7, 4, 8, 65536], P(None, 'gx', 'gy', 'gz'), as said below
- tile_lists: int32 [4, 8, 512, 8], P('gx', 'gy', 'gz'), may hold values from 0 to 63
- tile_counts: int32 [4, 8, 512], P('gx', 'gy', 'gz'), may hold values from 1 to 8, as said below
- ghost_counts: int32 [4, 8, 8, 4], P('gx', 'gy', 'gz'), may hold values from 1 to 12
- cell_index: int32 [4, 8, 65536], P('gx', 'gy', 'gz'), may hold values from 0 to 8191, as said below
- fluid_vel: float32 [3, 4, 8, 8192], P(None, 'gx', 'gy', 'gz'), may hold values from -6 to 6
- fluid_frac: float32 [4, 8, 8192], P('gx', 'gy', 'gz'), may hold values from 0.4 to 0.9
Outputs:
- velocity_new: float32 [3, 4, 8, 65536], P(None, 'gx', 'gy', 'gz')
- fluid_new: float32 [3, 4, 8, 8192], P(None, 'gx', 'gy', 'gz')
The draws below stay inside these ranges and needn't reach their ends.
Inputs may be any that keep to these rules, and one draw needn't show every extreme that they name: `state`: rows 0 to 2 are positions within 0 to 1, rows 3 to 5 velocities, row 6 radii within 0.15 to 0.35. `tile_counts`: in every box the first tile's count is the largest of that box. `cell_index`: A particle of box z along z has its cell in that box's slab, cells z * 1024 to (z + 1) * 1024 - 1, or in the slab of a box beside it along z.
All inputs are finite; a program needn't handle non-finite values.
Results may differ from the reference program's by a relative error of at most 0.0003.
Values sent between devices are 32-bit elements; how exact they have to be, the bound alone decides.
A program may use at most 64 MiB of HBM per device.

```python
import math
import jax
import jax.numpy as jnp
from jax import lax

TILE = 128
K = 8
NT = 64
FC_DEV = 1024
GB = 12
BOX_X = 4
BOX_Y = 8
BOX_Z = 8
TILES = 512
PARTS_SIZE = 65536
FLUID = 8192


def draw_state(key, part):
    key_pos = jax.random.fold_in(key, 101)
    key_vel = jax.random.fold_in(key, 102)
    key_rad = jax.random.fold_in(key, 103)
    positions = jax.random.uniform(key_pos, (3, BOX_X, BOX_Y, PARTS_SIZE), jnp.float32)
    velocity = jax.random.normal(key_vel, (3, BOX_X, BOX_Y, PARTS_SIZE), jnp.float32)
    radius = 0.15 * jnp.exp(jax.random.uniform(key_rad, (1, BOX_X, BOX_Y, PARTS_SIZE), jnp.float32) * math.log(0.35 / 0.15))
    return jnp.concatenate([positions, velocity, radius], axis=0).astype(jnp.float32)


def draw_tile_counts(key, part):
    key_level = jax.random.fold_in(key, 201)
    key_tiles = jax.random.fold_in(key, 202)
    level = jax.random.randint(key_level, (BOX_X, BOX_Y, BOX_Z, 1), 2, K + 1)
    level = level.at[0, 0, 0, 0].set(K)
    raw_draw = jax.random.randint(key_tiles, (BOX_X, BOX_Y, BOX_Z, NT), 0, 1048576)
    counts = 1 + raw_draw % level
    counts = counts.at[:, :, :, 0].set(level[:, :, :, 0])
    return counts.reshape(BOX_X, BOX_Y, BOX_Z * NT).astype(jnp.int32)


def draw_cell_index(key, part):
    key_side = jax.random.fold_in(key, 301)
    key_cell = jax.random.fold_in(key, 302)
    box_z = jnp.arange(PARTS_SIZE, dtype=jnp.int32) // (NT * TILE)
    roll = jax.random.randint(key_side, (BOX_X, BOX_Y, PARTS_SIZE), 0, 16)
    side = jnp.where(roll == 0, -1, jnp.where(roll == 1, 1, 0)).astype(jnp.int32)
    target = jnp.clip(box_z[None, None, :] + side, 0, BOX_Z - 1)
    offset = jax.random.randint(key_cell, (BOX_X, BOX_Y, PARTS_SIZE), 0, FC_DEV)
    return (target * FC_DEV + offset).astype(jnp.int32)


def plant(entries, rng, low, largest):
    extent = entries.shape
    place = [jax.random.randint(jax.random.fold_in(rng, axis), (), 0, extent[axis]) for axis in range(len(extent))]
    entries = entries.at[tuple(place)].set(low)
    longest = extent.index(max(extent))
    place[longest] = (place[longest] + 1) % extent[longest]
    return entries.at[tuple(place)].set(largest)


def block_scale(key, dims, cuts, low, largest):
    factor_of, own = 1.0, jax.random.fold_in(key, 6)
    for dim, blocks in cuts:
        draws = jnp.exp(jax.random.uniform(jax.random.fold_in(own, dim), (blocks,), jnp.float32, low / len(cuts), largest / len(cuts)))
        factor_of = factor_of * jnp.repeat(draws, dims[dim] // blocks).reshape([-1 if axis == dim else 1 for axis in range(len(dims))])
    return factor_of


def bell_draw(rng, extent, deviation, most, shards=(), kind=jnp.bfloat16):
    drawn = jax.random.normal(rng, extent, jnp.float32) * deviation
    if len(shards) > 0:
        drawn = block_scale(rng, extent, shards, -0.22, 0.18) * drawn
    return jnp.clip(drawn, min=-most, max=most).astype(kind)


def setup_inputs(seed: int = 0) -> dict:
    keys = jax.random.split(jax.random.key(seed), 8)
    state = draw_state(jax.random.fold_in(keys[7], 71), 0)
    tile_lists = plant(jax.random.randint(keys[1], (BOX_X, BOX_Y, TILES, K), 0, NT), jax.random.fold_in(keys[1], 1), 0, NT - 1).astype(jnp.int32)
    tile_counts = draw_tile_counts(jax.random.fold_in(keys[7], 71), 0)
    ghost_counts = plant(jax.random.randint(keys[3], (BOX_X, BOX_Y, BOX_Z, 4), 1, GB + 1), jax.random.fold_in(keys[3], 1), 1, GB).astype(jnp.int32)
    cell_index = draw_cell_index(jax.random.fold_in(keys[7], 71), 0)
    fluid_vel = bell_draw(keys[5], (3, BOX_X, BOX_Y, FLUID), 1.0, 6.0, ((1, 4), (2, 8), (3, 8)), jnp.float32)
    fluid_frac = jnp.clip(0.4 + 0.49999997 * jax.random.uniform(keys[6], (BOX_X, BOX_Y, FLUID), jnp.float32) ** block_scale(keys[6], (BOX_X, BOX_Y, FLUID), ((0, 4), (1, 8), (2, 8)), -0.2, 0.2), 0.4, 0.9)
    return dict(state=state, tile_lists=tile_lists, tile_counts=tile_counts, ghost_counts=ghost_counts, cell_index=cell_index, fluid_vel=fluid_vel, fluid_frac=fluid_frac)


stiffness = 5.0
damping = 2.0
time_step = 0.25
drag_coef = 64.0
fluid_density = 2.0
radius_ref = 0.25
highest = lax.Precision.HIGHEST


def pair_weight(near_tiles, far_tiles):
    offset = near_tiles[0][:, :, None] - far_tiles[0][:, None, :]
    distance = offset * offset
    for column in range(1, 3):
        offset = near_tiles[column][:, :, None] - far_tiles[column][:, None, :]
        distance = distance + offset * offset
    contact_reach = near_tiles[6][:, :, None] + far_tiles[6][:, None, :]
    return jnp.maximum(contact_reach * contact_reach - distance, 0.0) * near_tiles[7][:, :, None] * far_tiles[7][:, None, :]


def force_near(near_tiles, far_tiles, weight):
    totals = jnp.sum(weight, axis=2)
    weighted = jnp.einsum("tij,ctj->cti", weight, far_tiles[0:6], precision=highest)
    return stiffness * (near_tiles[0:3] * totals - weighted[0:3]) - damping * (near_tiles[3:6] * totals - weighted[3:6])


def face_block(tile_state, ghost_counts, face_index):
    border = tile_state[:, :, :, :, face_index * GB:(face_index + 1) * GB, :]
    living = (jnp.arange(GB, dtype=jnp.int32)[None, None, None, :] < ghost_counts[:, :, :, face_index:face_index + 1]).astype(jnp.float32)
    living = jnp.broadcast_to(living[None, :, :, :, :, None], (1,) + border.shape[1:])
    return jnp.concatenate([border, living], axis=0)


def shift_axis(blocked, along, upward):
    size_along = blocked.shape[along]
    zero_rim = jnp.zeros_like(lax.slice_in_dim(blocked, 0, 1, axis=along))
    if upward:
        return jnp.concatenate([zero_rim, lax.slice_in_dim(blocked, 0, size_along - 1, axis=along)], axis=along)
    return jnp.concatenate([lax.slice_in_dim(blocked, 1, size_along, axis=along), zero_rim], axis=along)


def box_forces(inputs):
    owned_tiles, tile_list, counts, face_tiles, ghosts = inputs

    def add_listed(listed, running):
        partner = jnp.take(owned_tiles, tile_list[:, listed], axis=1)
        weight = pair_weight(owned_tiles, partner)
        living = (listed < counts).astype(jnp.float32)
        return running + force_near(owned_tiles, partner, weight) * living[None, :, None]

    interior = lax.fori_loop(0, K, add_listed, jnp.zeros((3, NT, TILE), jnp.float32))
    across = force_near(face_tiles, ghosts, pair_weight(face_tiles, ghosts))
    return jnp.concatenate([interior[:, :4 * GB] + across, interior[:, 4 * GB:]], axis=1)


def reference(state, tile_lists, tile_counts, ghost_counts, cell_index, fluid_vel, fluid_frac):
    tile_state = state.reshape(7, BOX_X, BOX_Y, BOX_Z, NT, TILE)
    unit_rows = jnp.ones((1,) + tile_state.shape[1:], jnp.float32)
    owned_tiles = jnp.concatenate([tile_state, unit_rows], axis=0)
    face_list = [face_block(tile_state, ghost_counts, face_index) for face_index in range(4)]
    ghost_list = [shift_axis(face_list[1], 1, True), shift_axis(face_list[0], 1, False),
                  shift_axis(face_list[3], 2, True), shift_axis(face_list[2], 2, False)]
    face_tiles = jnp.concatenate(face_list, axis=4)
    ghosts = jnp.concatenate(ghost_list, axis=4)
    box_count = BOX_X * BOX_Y * BOX_Z

    def flatten_boxes(blocked):
        return jnp.moveaxis(blocked.reshape((blocked.shape[0], box_count) + blocked.shape[4:]), 1, 0)

    forces = lax.map(box_forces, (flatten_boxes(owned_tiles), tile_lists.reshape(box_count, NT, K),
                                  tile_counts.reshape(box_count, NT), flatten_boxes(face_tiles), flatten_boxes(ghosts)))
    columns = BOX_X * BOX_Y
    forces = jnp.moveaxis(forces, 0, 1).reshape(3, columns, PARTS_SIZE)
    velocity = state[3:6].reshape(3, columns, PARTS_SIZE)
    radius = state[6].reshape(1, columns, PARTS_SIZE)
    masses = (radius / radius_ref) ** 3
    drag_rate = drag_coef * radius * radius
    moved = velocity + time_step * forces / masses
    sources = jnp.concatenate([drag_rate * velocity, drag_rate], axis=0)
    cell_ids = cell_index.reshape(columns, PARTS_SIZE)

    def deposit(source, cell_row):
        return jax.ops.segment_sum(source.T, cell_row, num_segments=FLUID).T

    totals = jax.vmap(deposit, in_axes=(1, 0), out_axes=1)(sources, cell_ids)
    fraction = fluid_frac.reshape(1, columns, FLUID)
    previous = fluid_vel.reshape(3, columns, FLUID)
    fluid_new = (fluid_density * fraction * previous + time_step * totals[0:3]) / (fluid_density * fraction + time_step * totals[3:4])
    at_cell = jnp.take_along_axis(fluid_new, jnp.broadcast_to(cell_ids[None], (3, columns, PARTS_SIZE)), axis=2)
    coupling = time_step * drag_rate / masses
    velocity_new = (moved + coupling * at_cell) / (1.0 + coupling)
    return velocity_new.reshape(3, BOX_X, BOX_Y, PARTS_SIZE), fluid_new.reshape(3, BOX_X, BOX_Y, FLUID)
```

```python
import functools

import jax
import jax.numpy as jnp
from jax import lax
from jax.experimental import pallas as pl
from jax.experimental.pallas import tpu as pltpu
from jax.sharding import PartitionSpec as P

TILE = 128
K = 8
NT = 64
GB = 12
NB = 4 * GB
HI = 24
ROWS = 8

stiffness = 5.0
damping = 2.0
time_step = 0.25
drag_coef = 64.0
fluid_density = 2.0
radius_ref = 0.25
dead_level = -1.0e4

f32 = jnp.float32
bf16 = jnp.bfloat16
MESH = pl.DeviceIdType.MESH


def rounded(x):
    return x.astype(bf16).astype(f32)


def pieces(x):
    high = rounded(x)
    rest = x - high
    middle = rounded(rest)
    return high, middle, rounded(rest - middle)


def row_iota(shape):
    return lax.broadcasted_iota(jnp.int32, shape, 0)


def build_tile(tile, near_too, v8, table, near, ul):
    block = v8[pl.ds(pl.multiple_of(tile * ROWS, ROWS), ROWS), :]
    row = row_iota((ROWS, TILE))
    high, middle, low = pieces(block)
    shifted_middle = pltpu.roll(middle, 4, 0)
    one = jnp.float32(1.0)
    zero = jnp.float32(0.0)
    tail = jnp.where(row == 5, one, zero)
    far_high = jnp.where(row < 5, high, tail)
    far_middle = jnp.where(row < 5, middle, zero)
    far_low = jnp.where(row < 5, low, zero)
    stack = jnp.concatenate(
        [far_high, far_middle, far_high, far_middle, far_low, far_high] + [jnp.zeros((80, TILE), f32)], axis=0
    )
    table[tile] = stack.T.astype(bf16)
    first = jnp.where(row == 0, one, zero)
    ul[tile] = jnp.where(row >= 5, high, jnp.where((row >= 1) & (row <= 3), shifted_middle, first))
    if near_too:
        mark = jnp.where(row == 4, one, zero)

        def near_form(piece, fill):
            moved = pltpu.roll(piece, 1, 0)
            return jnp.where(row < 4, 2.0 * piece, jnp.where(row == 5, moved, fill))

        near_high = near_form(high, mark)
        near_middle = near_form(middle, zero)
        near_low = near_form(low, zero)
        stack = jnp.concatenate(
            [near_high, near_high, near_middle, near_middle, near_high, near_low] + [jnp.zeros((80, TILE), f32)],
            axis=0,
        )
        near[tile] = stack.astype(bf16)


def pair_sums(far_a, far_b, live_a, live_b, weights, table, ul):
    lhs = jnp.concatenate([table[far_a], table[far_b]], axis=1)
    weight = jnp.maximum(jnp.dot(lhs, weights, preferred_element_type=f32), 0.0)
    high = weight.astype(bf16)
    low = (weight - high.astype(f32)).astype(bf16)
    rows = jnp.concatenate([ul[far_a] * live_a, ul[far_b] * live_b], axis=0).astype(bf16)
    rows = jnp.concatenate([rows, rows], axis=1)
    return jnp.dot(rows, jnp.concatenate([high, low], axis=0), preferred_element_type=f32)


def near_weights(first, near):
    zero = jnp.zeros((TILE, TILE), bf16)
    upper = jnp.concatenate([near[first], zero], axis=1)
    lower = jnp.concatenate([zero, near[first + 1]], axis=1)
    return jnp.concatenate([upper, lower], axis=0)


def kernel(
    sizes,
    lists, counts, ghost_counts, state, cells, fluid_vel, fluid_frac,
    velocity_out, fluid_out,
    v8, send8, table, near, ul, sums, sources, onehot, deposit, slabs, arrived, window, at_cell,
    send_sem, recv_sem,
):
    names = ("gx", "gy", "gz")
    me = {name: lax.axis_index(name) for name in names}

    def beside(name, step):
        count = sizes[name]
        return {name: lax.rem(me[name] + step + count, count)}

    partners = [beside(name, step) for name in names for step in (-1, 1)]
    barrier = pltpu.get_barrier_semaphore()
    for partner in partners:
        pl.semaphore_signal(barrier, inc=1, device_id=partner, device_id_type=MESH)

    def remote(index, source, target, partner):
        return pltpu.make_async_remote_copy(
            src_ref=source, dst_ref=target, send_sem=send_sem.at[index], recv_sem=recv_sem.at[index],
            device_id=partner, device_id_type=MESH,
        )

    radius = state[6]
    masses = radius / radius_ref
    masses = masses * masses * masses
    drag_rate = drag_coef * radius * radius
    level = radius * radius
    for c in range(3):
        centred = state[c] - 0.5
        level = level - centred * centred
        v8[pl.ds(c, NT, stride=ROWS), :] = centred
        v8[pl.ds(5 + c, NT, stride=ROWS), :] = stiffness * centred - damping * state[3 + c]
    v8[pl.ds(3, NT, stride=ROWS), :] = radius
    v8[pl.ds(4, NT, stride=ROWS), :] = level

    row = row_iota((ROWS, TILE))
    for face in range(4):
        def copy_tile(j, carry, face=face):
            tile = face * GB + j
            place = pl.ds(pl.multiple_of(tile * ROWS, ROWS), ROWS)
            living = jnp.where(j < ghost_counts[face], 0.0, dead_level).astype(f32)
            block = v8[place, :]
            send8[place, :] = jnp.where(row == 4, jnp.where(living < -1.0, dead_level, block), block)
            return carry

        lax.fori_loop(0, GB, copy_tile, 0)

    pl.semaphore_wait(barrier, len(partners))

    width = GB * ROWS
    ghost_copies = []
    for face in range(4):
        name = names[face // 2]
        step = -1 if face % 2 == 0 else 1
        opposite = face ^ 1
        ghost_copies.append(
            remote(
                face,
                send8.at[pl.ds(face * width, width), :],
                v8.at[pl.ds(NT * ROWS + opposite * width, width), :],
                beside(name, step),
            )
        )
        ghost_copies[-1].start()

    for c in range(3):
        high = rounded(drag_rate * state[3 + c])
        sources[c] = high
        sources[4 + c] = rounded(drag_rate * state[3 + c] - high)
    high = rounded(drag_rate)
    sources[3] = high
    sources[7] = rounded(drag_rate - high)
    first_cell = (me["gz"] - 1) * (ROWS * TILE)
    step_tiles = 4
    deposit[...] = jnp.zeros_like(deposit)

    def add_chunk(chunk, carry):
        left, right = [], []
        for k in range(step_tiles):
            tile = chunk * step_tiles + k
            local = cells[pl.ds(tile, 1), :] - first_cell
            hot = (row_iota((TILE, TILE)) == (local & (TILE - 1))).astype(f32).astype(bf16)
            onehot[tile] = hot
            right.append(hot)
            mask = row_iota((HI, TILE)) == lax.shift_right_logical(local, 7)
            parts = [jnp.where(mask, sources[q, pl.ds(tile, 1), :], 0.0) for q in range(8)]
            left.append(jnp.concatenate(parts, axis=0).astype(bf16))
        deposit[...] += lax.dot_general(
            jnp.concatenate(left, axis=1), jnp.concatenate(right, axis=1),
            (((1,), (1,)), ((), ())), preferred_element_type=f32,
        )
        return carry

    lax.fori_loop(0, NT // step_tiles, add_chunk, 0)
    for q in range(4):
        both = deposit[pl.ds(q * HI, HI), :] + deposit[pl.ds((4 + q) * HI, HI), :]
        for slab in range(3):
            slabs[slab, q] = both[slab * ROWS:(slab + 1) * ROWS]

    slab_copies = [
        remote(4, slabs.at[0], arrived.at[1], beside("gz", -1)),
        remote(5, slabs.at[2], arrived.at[0], beside("gz", 1)),
    ]
    for copy in slab_copies:
        copy.start()

    def build_own(tile, carry):
        build_tile(tile, True, v8, table, near, ul)
        return carry

    lax.fori_loop(0, NT, build_own, 0)

    def near_pair(pair, carry):
        first = pair * 2
        weights = near_weights(first, near)
        total = jnp.zeros((2 * ROWS, 2 * TILE), f32)
        for s in range(K):
            live_a = jnp.where(s < counts[first], 1.0, 0.0).astype(f32)
            live_b = jnp.where(s < counts[first + 1], 1.0, 0.0).astype(f32)
            total = total + pair_sums(
                lists[first * K + s], lists[(first + 1) * K + s], live_a, live_b, weights, table, ul
            )
        sums[first] = total[0:ROWS, 0:TILE]
        sums[first + 1] = total[ROWS:, TILE:]
        return carry

    half = NT // 4
    lax.fori_loop(0, half, near_pair, 0)

    for copy in slab_copies:
        copy.wait()
    fraction = fluid_density * fluid_frac[...]
    below = fraction + time_step * (slabs[1, 3] + arrived[0, 3] + arrived[1, 3])
    for c in range(3):
        share = slabs[1, c] + arrived[0, c] + arrived[1, c]
        fresh = (fraction * fluid_vel[c] + time_step * share) / below
        window[1, c] = fresh
        fluid_out[c] = fresh
    fluid_copies = [
        remote(6, window.at[1], window.at[2], beside("gz", -1)),
        remote(7, window.at[1], window.at[0], beside("gz", 1)),
    ]
    for copy in fluid_copies:
        copy.start()

    lax.fori_loop(half, NT // 2, near_pair, 0)

    for copy in ghost_copies:
        copy.wait()

    def build_ghost(tile, carry):
        build_tile(NT + tile, False, v8, table, near, ul)
        return carry

    lax.fori_loop(0, NB, build_ghost, 0)
    for face in range(4):
        name = names[face // 2]
        edge = 0 if face % 2 == 0 else sizes[name] - 1
        inside = jnp.where(me[name] == edge, 0, 1)

        def ghost_pair(pair, carry, face=face, inside=inside):
            slot = pair * 2
            first = face * GB + slot
            limit = ghost_counts[face] * inside
            live_a = jnp.where(slot < limit, 1.0, 0.0).astype(f32)
            live_b = jnp.where(slot + 1 < limit, 1.0, 0.0).astype(f32)
            total = pair_sums(NT + first, NT + first + 1, live_a, live_b, near_weights(first, near), table, ul)
            sums[first] += total[0:ROWS, 0:TILE]
            sums[first + 1] += total[ROWS:, TILE:]
            return carry

        lax.fori_loop(0, GB // 2, ghost_pair, 0)

    for copy in fluid_copies:
        copy.wait()
    left = []
    for c in range(3):
        full = jnp.concatenate([window[0, c], window[1, c], window[2, c]], axis=0)
        high = rounded(full)
        left.append(jnp.concatenate([high, rounded(full - high)], axis=1))
    left = jnp.concatenate(left, axis=0).astype(bf16)

    def take_chunk(chunk, carry):
        hots = [onehot[chunk * step_tiles + k] for k in range(step_tiles)]
        hots = jnp.concatenate(hots, axis=1)
        spread = jnp.dot(left, jnp.concatenate([hots, hots], axis=0), preferred_element_type=f32)
        for k in range(step_tiles):
            tile = chunk * step_tiles + k
            local = cells[pl.ds(tile, 1), :] - first_cell
            mask = row_iota((HI, TILE)) == lax.shift_right_logical(local, 7)
            for c in range(3):
                part = jnp.where(mask, spread[c * HI:(c + 1) * HI, k * TILE:(k + 1) * TILE], 0.0)
                at_cell[c, pl.ds(tile, 1), :] = jnp.sum(part, axis=0, keepdims=True)
        return carry

    lax.fori_loop(0, NT // step_tiles, take_chunk, 0)

    coupling = time_step * drag_rate / masses
    per_mass = time_step / masses
    scale = 1.0 / (1.0 + coupling)
    total_weight = sums[:, 0, :]
    for c in range(3):
        speed = stiffness * (state[c] - 0.5) - damping * state[3 + c]
        high = rounded(speed)
        held = high + rounded(speed - high)
        force = held * total_weight - (sums[:, 5 + c, :] + sums[:, 1 + c, :])
        velocity_out[c] = (state[3 + c] + force * per_mass + coupling * at_cell[c]) * scale


def body(sizes, state, tile_lists, tile_counts, ghost_counts, cell_index, fluid_vel, fluid_frac):
    particles = state.shape[3]
    cell_count = fluid_vel.shape[3]
    vmem = pl.BlockSpec(memory_space=pltpu.VMEM)
    smem = pl.BlockSpec(memory_space=pltpu.SMEM)
    velocity, fluid = pl.pallas_call(
        functools.partial(kernel, sizes),
        out_shape=(
            jax.ShapeDtypeStruct((3, NT, TILE), f32),
            jax.ShapeDtypeStruct((3, ROWS, TILE), f32),
        ),
        in_specs=[smem, smem, smem, vmem, vmem, vmem, vmem],
        out_specs=(vmem, vmem),
        scratch_shapes=[
            pltpu.VMEM(((NT + NB) * ROWS, TILE), f32),
            pltpu.VMEM((NB * ROWS, TILE), f32),
            pltpu.VMEM((NT + NB, TILE, TILE), bf16),
            pltpu.VMEM((NT, TILE, TILE), bf16),
            pltpu.VMEM((NT + NB, ROWS, TILE), f32),
            pltpu.VMEM((NT, ROWS, TILE), f32),
            pltpu.VMEM((8, NT, TILE), f32),
            pltpu.VMEM((NT, TILE, TILE), bf16),
            pltpu.VMEM((8 * HI, TILE), f32),
            pltpu.VMEM((3, 4, ROWS, TILE), f32),
            pltpu.VMEM((2, 4, ROWS, TILE), f32),
            pltpu.VMEM((3, 3, ROWS, TILE), f32),
            pltpu.VMEM((3, NT, TILE), f32),
            pltpu.SemaphoreType.DMA((8,)),
            pltpu.SemaphoreType.DMA((8,)),
        ],
        compiler_params=pltpu.CompilerParams(
            collective_id=0, has_side_effects=True, vmem_limit_bytes=48 * 1024 * 1024
        ),
    )(
        tile_lists.reshape(NT * K),
        tile_counts.reshape(NT),
        ghost_counts.reshape(4),
        state.reshape(7, NT, TILE),
        cell_index.reshape(NT, TILE),
        fluid_vel.reshape(3, ROWS, TILE),
        fluid_frac.reshape(ROWS, TILE),
    )
    return velocity.reshape(3, 1, 1, particles), fluid.reshape(3, 1, 1, cell_count)


def solution(mesh):
    sizes = {name: mesh.shape[name] for name in ("gx", "gy", "gz")}
    return jax.shard_map(
        functools.partial(body, sizes),
        mesh=mesh,
        in_specs=(
            P(None, "gx", "gy", "gz"),
            P("gx", "gy", "gz", None),
            P("gx", "gy", "gz"),
            P("gx", "gy", "gz", None),
            P("gx", "gy", "gz"),
            P(None, "gx", "gy", "gz"),
            P("gx", "gy", "gz"),
        ),
        out_specs=(P(None, "gx", "gy", "gz"), P(None, "gx", "gy", "gz")),
        check_vma=False,
    )
```

```python
import functools

import jax
import jax.numpy as jnp
from jax import lax
from jax.experimental import pallas as pl
from jax.experimental.pallas import tpu as pltpu
from jax.sharding import PartitionSpec as P

TILE = 128
K = 8
NT = 64
GB = 12
NB = 4 * GB
HI = 24
ROWS = 8
DEPTH = 48
DEAD = NT + NB
GROUP = 4

stiffness = 5.0
damping = 2.0
time_step = 0.25
drag_coef = 64.0
fluid_density = 2.0
radius_ref = 0.25
dead_level = -8192.0

f32 = jnp.float32
bf16 = jnp.bfloat16
MESH = pl.DeviceIdType.MESH


def rounded(x):
    return x.astype(bf16).astype(f32)


def pieces(x):
    high = rounded(x)
    rest = x - high
    middle = rounded(rest)
    return high, middle, rounded(rest - middle)


def row_iota(shape):
    return lax.broadcasted_iota(jnp.int32, shape, 0)


def far_form(block):
    row = row_iota((ROWS, TILE))
    high, middle, low = pieces(block)
    one = jnp.where(row == 5, 1.0, 0.0).astype(f32)
    high = jnp.where(row < 5, high, one)
    middle = jnp.where(row < 5, middle, 0.0)
    low = jnp.where(row < 5, low, 0.0)
    return jnp.concatenate([high, middle, high, middle, low, high], axis=0).astype(bf16)


def near_form(block):
    row = row_iota((ROWS, TILE))
    one = jnp.where(row == 4, 1.0, 0.0).astype(f32)
    high, middle, low = [
        jnp.where(row < 4, 2.0 * piece, jnp.where(row == 5, pltpu.roll(piece, 1, 0), 0.0)) for piece in pieces(block)
    ]
    high = high + one
    return jnp.concatenate([high, high, middle, middle, high, low], axis=0)


def tile_sums(tile, far_tiles, near, far, v8):
    heights = jnp.concatenate([far[index] for index in far_tiles], axis=1)
    level = jnp.dot(near[tile][:, 0:DEPTH], heights, preferred_element_type=f32)
    weight = jnp.maximum(level, 0.0)
    totals = [None] * 4
    for s, index in enumerate(far_tiles):
        part = weight[:, s * TILE:(s + 1) * TILE].reshape(TILE // ROWS, ROWS, TILE)
        for q in range(4):
            term = part
            if q > 0:
                term = part * v8[pl.ds(index * ROWS + 4 + q, ROWS, stride=0), :][None]
            totals[q] = term if totals[q] is None else totals[q] + term
    return [jnp.sum(total.reshape(TILE, TILE), axis=1, keepdims=True) for total in totals]


def kernel(
    sizes,
    lists, counts, ghost_counts, state, cells, fluid_vel, fluid_frac,
    velocity_out, fluid_out,
    v8, send8, got8, near, far, sums, sources, onehot, deposit, slabs, arrived, window, at_cell,
    send_sem, recv_sem,
):
    names = ("gx", "gy", "gz")
    me = {name: lax.axis_index(name) for name in names}

    def beside(name, step):
        count = sizes[name]
        return {name: lax.rem(me[name] + step + count, count)}

    partners = [beside(name, step) for name in names for step in (-1, 1)]
    barrier = pltpu.get_barrier_semaphore()
    for partner in partners:
        pl.semaphore_signal(barrier, inc=1, device_id=partner, device_id_type=MESH)

    def remote(index, source, target, partner):
        return pltpu.make_async_remote_copy(
            src_ref=source, dst_ref=target, send_sem=send_sem.at[index], recv_sem=recv_sem.at[index],
            device_id=partner, device_id_type=MESH,
        )

    radius = state[6]
    masses = radius / radius_ref
    masses = masses * masses * masses
    drag_rate = drag_coef * radius * radius
    level = radius * radius
    for c in range(3):
        centred = state[c] - 0.5
        level = level - centred * centred
        v8[pl.ds(c, NT, stride=ROWS), :] = centred
        v8[pl.ds(5 + c, NT, stride=ROWS), :] = stiffness * centred - damping * state[3 + c]
    v8[pl.ds(3, NT, stride=ROWS), :] = radius
    v8[pl.ds(4, NT, stride=ROWS), :] = level

    send8[...] = v8[pl.ds(0, NB * ROWS), :]
    row = row_iota((NB, TILE))
    limit = jnp.where(row < GB, ghost_counts[0], GB + ghost_counts[1])
    limit = jnp.where(row < 2 * GB, limit, 2 * GB + ghost_counts[2])
    limit = jnp.where(row < 3 * GB, limit, 3 * GB + ghost_counts[3])
    send8[pl.ds(4, NB, stride=ROWS), :] = jnp.where(row < limit, level[0:NB], dead_level)
    row = row_iota((ROWS, TILE))
    v8[pl.ds(DEAD * ROWS, ROWS), :] = jnp.where(row == 4, dead_level, 0.0).astype(f32)

    pl.semaphore_wait(barrier, len(partners))

    width = GB * ROWS
    ghost_copies = []
    for face in range(4):
        name = names[face // 2]
        step = -1 if face % 2 == 0 else 1
        opposite = face ^ 1
        ghost_copies.append(
            remote(
                face,
                send8.at[pl.ds(face * width, width), :],
                got8.at[pl.ds(opposite * width, width), :],
                beside(name, step),
            )
        )
        ghost_copies[-1].start()

    for c in range(3):
        high = rounded(drag_rate * state[3 + c])
        sources[c] = high
        sources[4 + c] = rounded(drag_rate * state[3 + c] - high)
    high = rounded(drag_rate)
    sources[3] = high
    sources[7] = rounded(drag_rate - high)
    first_cell = (me["gz"] - 1) * (ROWS * TILE)
    step_tiles = 4
    deposit[...] = jnp.zeros_like(deposit)

    def add_chunk(chunk, carry):
        left, right = [], []
        for k in range(step_tiles):
            tile = chunk * step_tiles + k
            local = cells[pl.ds(tile, 1), :] - first_cell
            hot = (row_iota((TILE, TILE)) == (local & (TILE - 1))).astype(f32).astype(bf16)
            onehot[tile] = hot
            right.append(hot)
            mask = row_iota((HI, TILE)) == lax.shift_right_logical(local, 7)
            parts = [jnp.where(mask, sources[q, pl.ds(tile, 1), :], 0.0) for q in range(8)]
            left.append(jnp.concatenate(parts, axis=0).astype(bf16))
        deposit[...] += lax.dot_general(
            jnp.concatenate(left, axis=1), jnp.concatenate(right, axis=1),
            (((1,), (1,)), ((), ())), preferred_element_type=f32,
        )
        return carry

    lax.fori_loop(0, NT // step_tiles, add_chunk, 0)
    for q in range(4):
        both = deposit[pl.ds(q * HI, HI), :] + deposit[pl.ds((4 + q) * HI, HI), :]
        for slab in range(3):
            slabs[slab, q] = both[slab * ROWS:(slab + 1) * ROWS]

    slab_copies = [
        remote(4, slabs.at[0], arrived.at[1], beside("gz", -1)),
        remote(5, slabs.at[2], arrived.at[0], beside("gz", 1)),
    ]
    for copy in slab_copies:
        copy.start()

    def block_of(tile):
        return v8[pl.ds(pl.multiple_of(tile * ROWS, ROWS), ROWS), :]

    def build_own(group, carry):
        for k in range(GROUP):
            tile = group * GROUP + k
            block = block_of(tile)
            far[tile] = far_form(block)
            near[tile, :, 0:DEPTH] = near_form(block).T.astype(bf16)
        return carry

    lax.fori_loop(0, NT // GROUP, build_own, 0)
    far[DEAD] = far_form(block_of(DEAD))
    lane = lax.broadcasted_iota(jnp.int32, (TILE, TILE), 1)

    def listed(tile):
        return [jnp.where(s < counts[tile], lists[s, tile], DEAD) for s in range(K)]

    def near_group(group, extra):
        columns = []
        for k in range(GROUP):
            tile = group * GROUP + k
            columns.append((tile, tile_sums(tile, listed(tile) + extra(group, k), near, far, v8)))
        for q in range(4):
            held = sums[q]
            for tile, column in columns:
                held = jnp.where(lane == tile, column[q], held)
            sums[q] = held

    def inner_group(group, carry):
        near_group(group, lambda group, k: [])
        return carry

    lax.fori_loop(NB // GROUP, NT // GROUP, inner_group, 0)

    for copy in slab_copies:
        copy.wait()
    fraction = fluid_density * fluid_frac[...]
    below = fraction + time_step * (slabs[1, 3] + arrived[0, 3] + arrived[1, 3])
    for c in range(3):
        share = slabs[1, c] + arrived[0, c] + arrived[1, c]
        fresh = (fraction * fluid_vel[c] + time_step * share) / below
        window[1, c] = fresh
        fluid_out[c] = fresh
    fluid_copies = [
        remote(6, window.at[1], window.at[2], beside("gz", -1)),
        remote(7, window.at[1], window.at[0], beside("gz", 1)),
    ]
    for copy in fluid_copies:
        copy.start()

    for copy in ghost_copies:
        copy.wait()

    def build_ghost(group, carry):
        for k in range(GROUP):
            slot = pl.multiple_of((group * GROUP + k) * ROWS, ROWS)
            block = got8[pl.ds(slot, ROWS), :]
            v8[pl.ds(NT * ROWS + slot, ROWS), :] = block
            far[NT + group * GROUP + k] = far_form(block)
        return carry

    lax.fori_loop(0, NB // GROUP, build_ghost, 0)

    def ghost_of(face, inside):
        def extra(group, k):
            tile = group * GROUP + k
            return [jnp.where(tile - face * GB < ghost_counts[face] * inside, NT + tile, DEAD)]

        return extra

    for face in range(4):
        name = names[face // 2]
        edge = 0 if face % 2 == 0 else sizes[name] - 1
        inside = jnp.where(me[name] == edge, 0, 1)

        def border_group(group, carry, face=face, inside=inside):
            near_group(group, ghost_of(face, inside))
            return carry

        lax.fori_loop(face * GB // GROUP, (face + 1) * GB // GROUP, border_group, 0)

    for copy in fluid_copies:
        copy.wait()
    left = []
    for c in range(3):
        full = jnp.concatenate([window[0, c], window[1, c], window[2, c]], axis=0)
        high = rounded(full)
        left.append(jnp.concatenate([high, rounded(full - high)], axis=1))
    left = jnp.concatenate(left, axis=0).astype(bf16)

    def take_chunk(chunk, carry):
        hots = [onehot[chunk * step_tiles + k] for k in range(step_tiles)]
        hots = jnp.concatenate(hots, axis=1)
        spread = jnp.dot(left, jnp.concatenate([hots, hots], axis=0), preferred_element_type=f32)
        for k in range(step_tiles):
            tile = chunk * step_tiles + k
            local = cells[pl.ds(tile, 1), :] - first_cell
            mask = row_iota((HI, TILE)) == lax.shift_right_logical(local, 7)
            for c in range(3):
                part = jnp.where(mask, spread[c * HI:(c + 1) * HI, k * TILE:(k + 1) * TILE], 0.0)
                at_cell[c, pl.ds(tile, 1), :] = jnp.sum(part, axis=0, keepdims=True)
        return carry

    lax.fori_loop(0, NT // step_tiles, take_chunk, 0)

    coupling = time_step * drag_rate / masses
    per_mass = time_step / masses
    scale = 1.0 / (1.0 + coupling)
    total_weight = sums[0].T[0:NT]
    for c in range(3):
        speed = stiffness * (state[c] - 0.5) - damping * state[3 + c]
        force = speed * total_weight - sums[1 + c].T[0:NT]
        velocity_out[c] = (state[3 + c] + force * per_mass + coupling * at_cell[c]) * scale


def body(sizes, state, tile_lists, tile_counts, ghost_counts, cell_index, fluid_vel, fluid_frac):
    particles = state.shape[3]
    cell_count = fluid_vel.shape[3]
    vmem = pl.BlockSpec(memory_space=pltpu.VMEM)
    smem = pl.BlockSpec(memory_space=pltpu.SMEM)
    velocity, fluid = pl.pallas_call(
        functools.partial(kernel, sizes),
        out_shape=(
            jax.ShapeDtypeStruct((3, NT, TILE), f32),
            jax.ShapeDtypeStruct((3, ROWS, TILE), f32),
        ),
        in_specs=[smem, smem, smem, vmem, vmem, vmem, vmem],
        out_specs=(vmem, vmem),
        scratch_shapes=[
            pltpu.VMEM(((DEAD + 1) * ROWS, TILE), f32),
            pltpu.VMEM((NB * ROWS, TILE), f32),
            pltpu.VMEM((NB * ROWS, TILE), f32),
            pltpu.VMEM((NT, TILE, TILE), bf16),
            pltpu.VMEM((DEAD + 1, DEPTH, TILE), bf16),
            pltpu.VMEM((4, TILE, TILE), f32),
            pltpu.VMEM((8, NT, TILE), f32),
            pltpu.VMEM((NT, TILE, TILE), bf16),
            pltpu.VMEM((8 * HI, TILE), f32),
            pltpu.VMEM((3, 4, ROWS, TILE), f32),
            pltpu.VMEM((2, 4, ROWS, TILE), f32),
            pltpu.VMEM((3, 3, ROWS, TILE), f32),
            pltpu.VMEM((3, NT, TILE), f32),
            pltpu.SemaphoreType.DMA((8,)),
            pltpu.SemaphoreType.DMA((8,)),
        ],
        compiler_params=pltpu.CompilerParams(
            collective_id=0, has_side_effects=True, vmem_limit_bytes=48 * 1024 * 1024
        ),
    )(
        tile_lists.reshape(NT, K).T,
        tile_counts.reshape(NT),
        ghost_counts.reshape(4),
        state.reshape(7, NT, TILE),
        cell_index.reshape(NT, TILE),
        fluid_vel.reshape(3, ROWS, TILE),
        fluid_frac.reshape(ROWS, TILE),
    )
    return velocity.reshape(3, 1, 1, particles), fluid.reshape(3, 1, 1, cell_count)


def solution(mesh):
    sizes = {name: mesh.shape[name] for name in ("gx", "gy", "gz")}
    return jax.shard_map(
        functools.partial(body, sizes),
        mesh=mesh,
        in_specs=(
            P(None, "gx", "gy", "gz"),
            P("gx", "gy", "gz", None),
            P("gx", "gy", "gz"),
            P("gx", "gy", "gz", None),
            P("gx", "gy", "gz"),
            P(None, "gx", "gy", "gz"),
            P("gx", "gy", "gz"),
        ),
        out_specs=(P(None, "gx", "gy", "gz"), P(None, "gx", "gy", "gz")),
        check_vma=False,
    )
```

```python
import functools

import jax
import jax.numpy as jnp
from jax import lax
from jax.experimental import pallas as pl
from jax.experimental.pallas import tpu as pltpu
from jax.sharding import PartitionSpec as P

TILE = 128
K = 8
NT = 64
GB = 12
NB = 4 * GB
HI = 24
ROWS = 8
DEPTH = 16
DEAD = NT + NB
GROUP = 4
UNROLL = 8

stiffness = 5.0
damping = 2.0
time_step = 0.25
drag_coef = 64.0
fluid_density = 2.0
radius_ref = 0.25
dead_level = -8192.0

f32 = jnp.float32
bf16 = jnp.bfloat16
MESH = pl.DeviceIdType.MESH


def rounded(x):
    return x.astype(bf16).astype(f32)


def pieces(x):
    high = rounded(x)
    return high, rounded(x - high)


def row_iota(shape):
    return lax.broadcasted_iota(jnp.int32, shape, 0)


def far_form(block):
    row = row_iota((ROWS, TILE))
    high, middle = pieces(block)
    first = jnp.where(row < 4, high, pltpu.roll(middle, 4, 0))
    second = jnp.where(row < 5, high, jnp.where(row == 5, pltpu.roll(middle, 1, 0), 1.0))
    return jnp.concatenate([first, second], axis=0).astype(bf16)


def near_form(block):
    row = row_iota((ROWS, TILE))
    high, middle = pieces(block)
    first = 2.0 * jnp.where(row < 4, high, pltpu.roll(high, 4, 0))
    level = jnp.where(row == 6, pltpu.roll(high, 2, 0), pltpu.roll(middle, 3, 0))
    second = jnp.where(row < 4, 2.0 * middle, jnp.where(row < 6, 1.0, level))
    return jnp.concatenate([first, second], axis=0)


def set_levels(tile, far_tiles, near, far, levels):
    heights = jnp.concatenate([far[index] for index in far_tiles], axis=1)
    width = len(far_tiles) * TILE
    levels[:, 0:width] = jnp.dot(near[tile][:, 0:DEPTH], heights, preferred_element_type=f32)


def add_far(far_tiles, v8, levels, totals):
    pulls = [[v8[pl.ds(index * ROWS + 5 + c, ROWS, stride=0), :] for c in range(3)] for index in far_tiles]
    for r in range(0, TILE, ROWS):
        held = [None] * 4
        for s, pull in enumerate(pulls):
            weight = jnp.maximum(levels[r:r + ROWS, s * TILE:(s + 1) * TILE], 0.0)
            terms = [weight] + [weight * row for row in pull]
            held = [term if total is None else total + term for total, term in zip(held, terms)]
        for q in range(4):
            totals[q, r:r + ROWS, :] = held[q]


def sum_lanes(tile, totals, sums):
    mask = lax.broadcasted_iota(jnp.int32, (ROWS, TILE), 1) == tile
    for q in range(4):
        for r in range(0, TILE, ROWS):
            column = jnp.sum(totals[q, r:r + ROWS, :], axis=1, keepdims=True)
            pltpu.store(sums.at[q, r:r + ROWS, :], jnp.broadcast_to(column, (ROWS, TILE)), mask=mask)


def kernel(
    sizes,
    lists_in, counts_in, ghost_counts_in, state_in, cells_in, fluid_vel_in, fluid_frac_in,
    velocity_out, fluid_out,
    lists, counts, ghost_counts, state, cells, fluid_vel, fluid_frac,
    v8, send8, got8, near, far, levels, totals, sums, sources, onehot, deposit, slabs, arrived, window, at_cell,
    send_sem, recv_sem, in_sem,
):
    loads = [
        pltpu.make_async_copy(source, target, in_sem.at[index])
        for index, (source, target) in enumerate([
            (state_in, state), (ghost_counts_in, ghost_counts), (cells_in, cells), (lists_in, lists),
            (counts_in, counts), (fluid_vel_in, fluid_vel), (fluid_frac_in, fluid_frac),
        ])
    ]
    for load in loads:
        load.start()
    names = ("gx", "gy", "gz")
    me = {name: lax.axis_index(name) for name in names}

    def beside(name, step):
        count = sizes[name]
        return {name: lax.rem(me[name] + step + count, count)}

    partners = [beside(name, step) for name in names for step in (-1, 1)]
    barrier = pltpu.get_barrier_semaphore()
    for partner in partners:
        pl.semaphore_signal(barrier, inc=1, device_id=partner, device_id_type=MESH)

    def remote(index, source, target, partner):
        return pltpu.make_async_remote_copy(
            src_ref=source, dst_ref=target, send_sem=send_sem.at[index], recv_sem=recv_sem.at[index],
            device_id=partner, device_id_type=MESH,
        )

    for load in loads:
        load.wait()
    radius = state[6]
    masses = radius / radius_ref
    masses = masses * masses * masses
    drag_rate = drag_coef * radius * radius
    level = radius * radius
    for c in range(3):
        centred = state[c] - 0.5
        level = level - centred * centred
        v8[pl.ds(c, NT, stride=ROWS), :] = centred
        v8[pl.ds(5 + c, NT, stride=ROWS), :] = stiffness * centred - damping * state[3 + c]
    v8[pl.ds(3, NT, stride=ROWS), :] = radius
    v8[pl.ds(4, NT, stride=ROWS), :] = level

    send8[...] = v8[pl.ds(0, NB * ROWS), :]
    row = row_iota((NB, TILE))
    limit = jnp.where(row < GB, ghost_counts[0], GB + ghost_counts[1])
    limit = jnp.where(row < 2 * GB, limit, 2 * GB + ghost_counts[2])
    limit = jnp.where(row < 3 * GB, limit, 3 * GB + ghost_counts[3])
    send8[pl.ds(4, NB, stride=ROWS), :] = jnp.where(row < limit, level[0:NB], dead_level)
    row = row_iota((ROWS, TILE))
    v8[pl.ds(DEAD * ROWS, ROWS), :] = jnp.where(row == 4, dead_level, 0.0).astype(f32)

    pl.semaphore_wait(barrier, len(partners))

    width = GB * ROWS
    ghost_copies = []
    for face in range(4):
        name = names[face // 2]
        step = -1 if face % 2 == 0 else 1
        opposite = face ^ 1
        ghost_copies.append(
            remote(
                face,
                send8.at[pl.ds(face * width, width), :],
                got8.at[pl.ds(opposite * width, width), :],
                beside(name, step),
            )
        )
        ghost_copies[-1].start()

    for c in range(3):
        high = rounded(drag_rate * state[3 + c])
        sources[c] = high
        sources[4 + c] = rounded(drag_rate * state[3 + c] - high)
    high = rounded(drag_rate)
    sources[3] = high
    sources[7] = rounded(drag_rate - high)
    first_cell = (me["gz"] - 1) * (ROWS * TILE)
    step_tiles = 16
    deposit[...] = jnp.zeros_like(deposit)

    def add_chunk(chunk, carry):
        left, right = [], []
        for k in range(step_tiles):
            tile = chunk * step_tiles + k
            local = cells[pl.ds(tile, 1), :] - first_cell
            hot = (row_iota((TILE, TILE)) == (local & (TILE - 1))).astype(f32).astype(bf16)
            onehot[tile] = hot
            right.append(hot)
            mask = row_iota((HI, TILE)) == lax.shift_right_logical(local, 7)
            parts = [jnp.where(mask, sources[q, pl.ds(tile, 1), :], 0.0) for q in range(8)]
            left.append(jnp.concatenate(parts, axis=0).astype(bf16))
        deposit[...] += lax.dot_general(
            jnp.concatenate(left, axis=1), jnp.concatenate(right, axis=1),
            (((1,), (1,)), ((), ())), preferred_element_type=f32,
        )
        return carry

    lax.fori_loop(0, NT // step_tiles, add_chunk, 0)
    for q in range(4):
        both = deposit[pl.ds(q * HI, HI), :] + deposit[pl.ds((4 + q) * HI, HI), :]
        for slab in range(3):
            slabs[slab, q] = both[slab * ROWS:(slab + 1) * ROWS]

    slab_copies = [
        remote(4, slabs.at[0], arrived.at[1], beside("gz", -1)),
        remote(5, slabs.at[2], arrived.at[0], beside("gz", 1)),
    ]
    for copy in slab_copies:
        copy.start()

    def block_of(tile):
        return v8[pl.ds(pl.multiple_of(tile * ROWS, ROWS), ROWS), :]

    def build_own(group, carry):
        for k in range(GROUP):
            tile = group * GROUP + k
            block = block_of(tile)
            far[tile] = far_form(block)
            near[tile, :, 0:DEPTH] = near_form(block).T.astype(bf16)
        return carry

    lax.fori_loop(0, NT // GROUP, build_own, 0)
    far[DEAD] = far_form(block_of(DEAD))
    def listed(tile):
        return [jnp.where(s < counts[tile], lists[s, tile], DEAD) for s in range(K)]

    def sweep(first, last, listing):
        set_levels(first, listing(first), near, far, levels.at[0])
        totals[1] = jnp.zeros((4, TILE, TILE), f32)

        def some_tiles(group, carry):
            for k in range(UNROLL):
                tile = first + UNROLL * group + k
                now, later = k % 2, (k + 1) % 2
                before = tile - 1 if k > 0 else jnp.where(group == 0, -1, tile - 1)
                after = tile + 1 if k < UNROLL - 1 else jnp.minimum(tile + 1, last - 1)
                add_far(listing(tile), v8, levels.at[now], totals.at[now])
                set_levels(after, listing(after), near, far, levels.at[later])
                sum_lanes(before, totals.at[later], sums)
            return carry

        lax.fori_loop(0, (last - first) // UNROLL, some_tiles, 0)
        sum_lanes(last - 1, totals.at[1], sums)

    sweep(NB, NT, listed)

    for copy in slab_copies:
        copy.wait()
    fraction = fluid_density * fluid_frac[...]
    below = fraction + time_step * (slabs[1, 3] + arrived[0, 3] + arrived[1, 3])
    for c in range(3):
        share = slabs[1, c] + arrived[0, c] + arrived[1, c]
        fresh = (fraction * fluid_vel[c] + time_step * share) / below
        window[1, c] = fresh
        fluid_out[c] = fresh
    fluid_copies = [
        remote(6, window.at[1], window.at[2], beside("gz", -1)),
        remote(7, window.at[1], window.at[0], beside("gz", 1)),
    ]
    for copy in fluid_copies:
        copy.start()

    for copy in ghost_copies:
        copy.wait()

    def build_ghost(group, carry):
        for k in range(GROUP):
            slot = pl.multiple_of((group * GROUP + k) * ROWS, ROWS)
            block = got8[pl.ds(slot, ROWS), :]
            v8[pl.ds(NT * ROWS + slot, ROWS), :] = block
            far[NT + group * GROUP + k] = far_form(block)
        return carry

    lax.fori_loop(0, NB // GROUP, build_ghost, 0)
    limits = []
    for face in range(4):
        name = names[face // 2]
        edge = 0 if face % 2 == 0 else sizes[name] - 1
        limits.append(face * GB + jnp.where(me[name] == edge, 0, ghost_counts[face]))

    def listed_too(tile):
        limit = jnp.where(tile < 2 * GB, jnp.where(tile < GB, limits[0], limits[1]),
                          jnp.where(tile < 3 * GB, limits[2], limits[3]))
        return listed(tile) + [jnp.where(tile < limit, NT + tile, DEAD)]

    sweep(0, NB, listed_too)

    for copy in fluid_copies:
        copy.wait()
    left = []
    for c in range(3):
        full = jnp.concatenate([window[0, c], window[1, c], window[2, c]], axis=0)
        high = rounded(full)
        left.append(jnp.concatenate([high, rounded(full - high)], axis=1))
    left = jnp.concatenate(left, axis=0).astype(bf16)

    def take_chunk(chunk, carry):
        hots = [onehot[chunk * step_tiles + k] for k in range(step_tiles)]
        hots = jnp.concatenate(hots, axis=1)
        spread = jnp.dot(left, jnp.concatenate([hots, hots], axis=0), preferred_element_type=f32)
        for k in range(step_tiles):
            tile = chunk * step_tiles + k
            local = cells[pl.ds(tile, 1), :] - first_cell
            mask = row_iota((HI, TILE)) == lax.shift_right_logical(local, 7)
            for c in range(3):
                part = jnp.where(mask, spread[c * HI:(c + 1) * HI, k * TILE:(k + 1) * TILE], 0.0)
                at_cell[c, pl.ds(tile, 1), :] = jnp.sum(part, axis=0, keepdims=True)
        return carry

    lax.fori_loop(0, NT // step_tiles, take_chunk, 0)

    coupling = time_step * drag_rate / masses
    per_mass = time_step / masses
    scale = 1.0 / (1.0 + coupling)
    def row_form(q):
        return sums[q].T[0:NT]

    total_weight = row_form(0)
    for c in range(3):
        speed = stiffness * (state[c] - 0.5) - damping * state[3 + c]
        force = speed * total_weight - row_form(1 + c)
        velocity_out[c] = (state[3 + c] + force * per_mass + coupling * at_cell[c]) * scale


def body(sizes, state, tile_lists, tile_counts, ghost_counts, cell_index, fluid_vel, fluid_frac):
    particles = state.shape[3]
    cell_count = fluid_vel.shape[3]
    vmem = pl.BlockSpec(memory_space=pltpu.VMEM)
    hbm = pl.BlockSpec(memory_space=pltpu.HBM)
    velocity, fluid = pl.pallas_call(
        functools.partial(kernel, sizes),
        out_shape=(
            jax.ShapeDtypeStruct((3, NT, TILE), f32),
            jax.ShapeDtypeStruct((3, ROWS, TILE), f32),
        ),
        in_specs=[hbm] * 7,
        out_specs=(vmem, vmem),
        scratch_shapes=[
            pltpu.SMEM((K, NT), jnp.int32),
            pltpu.SMEM((NT,), jnp.int32),
            pltpu.SMEM((4,), jnp.int32),
            pltpu.VMEM((7, NT, TILE), f32),
            pltpu.VMEM((NT, TILE), jnp.int32),
            pltpu.VMEM((3, ROWS, TILE), f32),
            pltpu.VMEM((ROWS, TILE), f32),
            pltpu.VMEM(((DEAD + 1) * ROWS, TILE), f32),
            pltpu.VMEM((NB * ROWS, TILE), f32),
            pltpu.VMEM((NB * ROWS, TILE), f32),
            pltpu.VMEM((NT, TILE, TILE), bf16),
            pltpu.VMEM((DEAD + 1, DEPTH, TILE), bf16),
            pltpu.VMEM((2, TILE, (K + 1) * TILE), f32),
            pltpu.VMEM((2, 4, TILE, TILE), f32),
            pltpu.VMEM((4, TILE, TILE), f32),
            pltpu.VMEM((8, NT, TILE), f32),
            pltpu.VMEM((NT, TILE, TILE), bf16),
            pltpu.VMEM((8 * HI, TILE), f32),
            pltpu.VMEM((3, 4, ROWS, TILE), f32),
            pltpu.VMEM((2, 4, ROWS, TILE), f32),
            pltpu.VMEM((3, 3, ROWS, TILE), f32),
            pltpu.VMEM((3, NT, TILE), f32),
            pltpu.SemaphoreType.DMA((8,)),
            pltpu.SemaphoreType.DMA((8,)),
            pltpu.SemaphoreType.DMA((7,)),
        ],
        compiler_params=pltpu.CompilerParams(
            collective_id=0, has_side_effects=True, vmem_limit_bytes=64 * 1024 * 1024
        ),
    )(
        tile_lists.reshape(NT, K).T,
        tile_counts.reshape(NT),
        ghost_counts.reshape(4),
        state.reshape(7, NT, TILE),
        cell_index.reshape(NT, TILE),
        fluid_vel.reshape(3, ROWS, TILE),
        fluid_frac.reshape(ROWS, TILE),
    )
    return velocity.reshape(3, 1, 1, particles), fluid.reshape(3, 1, 1, cell_count)


def solution(mesh):
    sizes = {name: mesh.shape[name] for name in ("gx", "gy", "gz")}
    return jax.shard_map(
        functools.partial(body, sizes),
        mesh=mesh,
        in_specs=(
            P(None, "gx", "gy", "gz"),
            P("gx", "gy", "gz", None),
            P("gx", "gy", "gz"),
            P("gx", "gy", "gz", None),
            P("gx", "gy", "gz"),
            P(None, "gx", "gy", "gz"),
            P("gx", "gy", "gz"),
        ),
        out_specs=(P(None, "gx", "gy", "gz"), P(None, "gx", "gy", "gz")),
        check_vma=False,
    )
```

```python
import functools

import jax
import jax.numpy as jnp
from jax import lax
from jax.experimental import pallas as pl
from jax.experimental.pallas import tpu as pltpu
from jax.sharding import PartitionSpec as P

TILE = 128
K = 8
NT = 64
GB = 12
NB = 4 * GB
HI = 24
ROWS = 8
DEPTH = 16
DEAD = NT + NB
GROUP = 4
UNROLL = 8

stiffness = 5.0
damping = 2.0
time_step = 0.25
drag_coef = 64.0
fluid_density = 2.0
radius_ref = 0.25
dead_level = -8192.0

f32 = jnp.float32
bf16 = jnp.bfloat16
MESH = pl.DeviceIdType.MESH


def rounded(x):
    return x.astype(bf16).astype(f32)


def pieces(x):
    high = rounded(x)
    return high, rounded(x - high)


def row_iota(shape):
    return lax.broadcasted_iota(jnp.int32, shape, 0)


def far_form(block):
    row = row_iota((ROWS, TILE))
    high, middle = pieces(block)
    first = jnp.where(row < 4, high, pltpu.roll(middle, 4, 0))
    second = jnp.where(row < 5, high, jnp.where(row == 5, pltpu.roll(middle, 1, 0), 1.0))
    return jnp.concatenate([first, second], axis=0).astype(bf16)


def near_form(block):
    row = row_iota((ROWS, TILE))
    high, middle = pieces(block)
    first = 2.0 * jnp.where(row < 4, high, pltpu.roll(high, 4, 0))
    level = jnp.where(row == 6, pltpu.roll(high, 2, 0), pltpu.roll(middle, 3, 0))
    second = jnp.where(row < 4, 2.0 * middle, jnp.where(row < 6, 1.0, level))
    return jnp.concatenate([first, second], axis=0)


def set_levels(tile, far_tiles, near, far, levels):
    heights = jnp.concatenate([far[index] for index in far_tiles], axis=1)
    width = len(far_tiles) * TILE
    rows = near[tile][:, 0:DEPTH]
    levels[:, 0:width] = jnp.dot(rows, heights, preferred_element_type=f32)


def add_far(far_tiles, v8, levels, totals):
    pulls = [[v8[pl.ds(index * ROWS + 5 + c, ROWS, stride=0), :] for c in range(3)] for index in far_tiles]
    for r in range(0, TILE, ROWS):
        held = [None] * 4
        for s, pull in enumerate(pulls):
            weight = jnp.maximum(levels[r:r + ROWS, s * TILE:(s + 1) * TILE], 0.0)
            terms = [weight] + [weight * row for row in pull]
            held = [term if total is None else total + term for total, term in zip(held, terms)]
        for q in range(4):
            totals[q, r:r + ROWS, :] = held[q]


def sum_lanes(tile, totals, sums):
    mask = lax.broadcasted_iota(jnp.int32, (ROWS, TILE), 1) == tile
    for q in range(4):
        for r in range(0, TILE, ROWS):
            column = jnp.sum(totals[q, r:r + ROWS, :], axis=1, keepdims=True)
            pltpu.store(sums.at[q, r:r + ROWS, :], jnp.broadcast_to(column, (ROWS, TILE)), mask=mask)


def kernel(
    sizes,
    lists_in, counts_in, ghost_counts_in, state_in, cells_in, fluid_vel_in, fluid_frac_in,
    velocity_out, fluid_out,
    lists, counts, ghost_counts, state, cells, fluid_vel, fluid_frac,
    v8, send8, got8, near, far, levels, totals, sums, sources, onehot, deposit, slabs, arrived, window, at_cell,
    send_sem, recv_sem, in_sem,
):
    loads = [
        pltpu.make_async_copy(source, target, in_sem.at[index])
        for index, (source, target) in enumerate([
            (state_in, state), (ghost_counts_in, ghost_counts), (cells_in, cells), (lists_in, lists),
            (counts_in, counts), (fluid_vel_in, fluid_vel), (fluid_frac_in, fluid_frac),
        ])
    ]
    for load in loads:
        load.start()
    names = ("gx", "gy", "gz")
    me = {name: lax.axis_index(name) for name in names}

    def beside(name, step):
        count = sizes[name]
        return {name: lax.rem(me[name] + step + count, count)}

    partners = [beside(name, step) for name in names for step in (-1, 1)]
    barrier = pltpu.get_barrier_semaphore()
    for partner in partners:
        pl.semaphore_signal(barrier, inc=1, device_id=partner, device_id_type=MESH)

    def remote(index, source, target, partner):
        return pltpu.make_async_remote_copy(
            src_ref=source, dst_ref=target, send_sem=send_sem.at[index], recv_sem=recv_sem.at[index],
            device_id=partner, device_id_type=MESH,
        )

    for load in loads:
        load.wait()
    radius = state[6]
    masses = radius / radius_ref
    masses = masses * masses * masses
    drag_rate = drag_coef * radius * radius
    level = radius * radius
    for c in range(3):
        centred = state[c] - 0.5
        level = level - centred * centred
        v8[pl.ds(c, NT, stride=ROWS), :] = centred
        v8[pl.ds(5 + c, NT, stride=ROWS), :] = stiffness * centred - damping * state[3 + c]
    v8[pl.ds(3, NT, stride=ROWS), :] = radius
    v8[pl.ds(4, NT, stride=ROWS), :] = level

    send8[...] = v8[pl.ds(0, NB * ROWS), :]
    row = row_iota((NB, TILE))
    limit = jnp.where(row < GB, ghost_counts[0], GB + ghost_counts[1])
    limit = jnp.where(row < 2 * GB, limit, 2 * GB + ghost_counts[2])
    limit = jnp.where(row < 3 * GB, limit, 3 * GB + ghost_counts[3])
    send8[pl.ds(4, NB, stride=ROWS), :] = jnp.where(row < limit, level[0:NB], dead_level)
    row = row_iota((ROWS, TILE))
    v8[pl.ds(DEAD * ROWS, ROWS), :] = jnp.where(row == 4, dead_level, 0.0).astype(f32)

    for c in range(3):
        high = rounded(drag_rate * state[3 + c])
        sources[c] = high
        sources[4 + c] = rounded(drag_rate * state[3 + c] - high)
    high = rounded(drag_rate)
    sources[3] = high
    sources[7] = rounded(drag_rate - high)
    first_cell = (me["gz"] - 1) * (ROWS * TILE)
    step_tiles = 16
    deposit[...] = jnp.zeros_like(deposit)

    places = row_iota((TILE, TILE)).astype(f32).astype(bf16)

    def add_chunk(chunk, carry):
        left, right = [], []
        for k in range(step_tiles):
            tile = chunk * step_tiles + k
            local = cells[pl.ds(tile, 1), :] - first_cell
            low = (local & (TILE - 1)).astype(f32).astype(bf16)
            hot = jnp.where(places == low, jnp.ones((), bf16), jnp.zeros((), bf16))
            onehot[tile] = hot
            right.append(hot)
            mask = row_iota((HI, TILE)) == lax.shift_right_logical(local, 7)
            parts = [jnp.where(mask, sources[q, pl.ds(tile, 1), :], 0.0) for q in range(8)]
            left.append(jnp.concatenate(parts, axis=0).astype(bf16))
        deposit[...] += lax.dot_general(
            jnp.concatenate(left, axis=1), jnp.concatenate(right, axis=1),
            (((1,), (1,)), ((), ())), preferred_element_type=f32,
        )
        return carry

    lax.fori_loop(0, NT // step_tiles, add_chunk, 0)
    for q in range(4):
        both = deposit[pl.ds(q * HI, HI), :] + deposit[pl.ds((4 + q) * HI, HI), :]
        for slab in range(3):
            slabs[slab, q] = both[slab * ROWS:(slab + 1) * ROWS]

    pl.semaphore_wait(barrier, len(partners))

    width = GB * ROWS
    ghost_copies = []
    for face in range(4):
        name = names[face // 2]
        step = -1 if face % 2 == 0 else 1
        opposite = face ^ 1
        ghost_copies.append(
            remote(
                face,
                send8.at[pl.ds(face * width, width), :],
                got8.at[pl.ds(opposite * width, width), :],
                beside(name, step),
            )
        )
        ghost_copies[-1].start()

    slab_copies = [
        remote(4, slabs.at[0], arrived.at[1], beside("gz", -1)),
        remote(5, slabs.at[2], arrived.at[0], beside("gz", 1)),
    ]
    for copy in slab_copies:
        copy.start()

    def block_of(tile):
        return v8[pl.ds(pl.multiple_of(tile * ROWS, ROWS), ROWS), :]

    def build_own(group, carry):
        for k in range(GROUP):
            tile = group * GROUP + k
            block = block_of(tile)
            far[tile] = far_form(block)
            near[tile, :, 0:DEPTH] = near_form(block).T.astype(bf16)
        return carry

    lax.fori_loop(0, NT // GROUP, build_own, 0)
    far[DEAD] = far_form(block_of(DEAD))
    def listed(tile):
        return [jnp.where(s < counts[tile], lists[s, tile], DEAD) for s in range(K)]

    def sweep(first, last, listing):
        set_levels(first, listing(first), near, far, levels.at[0])
        totals[1] = jnp.zeros((4, TILE, TILE), f32)

        def some_tiles(group, carry):
            for k in range(UNROLL):
                tile = first + UNROLL * group + k
                now, later = k % 2, (k + 1) % 2
                before = tile - 1 if k > 0 else jnp.where(group == 0, -1, tile - 1)
                after = tile + 1 if k < UNROLL - 1 else jnp.minimum(tile + 1, last - 1)
                add_far(listing(tile), v8, levels.at[now], totals.at[now])
                set_levels(after, listing(after), near, far, levels.at[later])
                sum_lanes(before, totals.at[later], sums)
            return carry

        lax.fori_loop(0, (last - first) // UNROLL, some_tiles, 0)
        sum_lanes(last - 1, totals.at[1], sums)

    sweep(NB, NT, listed)

    for copy in slab_copies:
        copy.wait()
    fraction = fluid_density * fluid_frac[...]
    below = fraction + time_step * (slabs[1, 3] + arrived[0, 3] + arrived[1, 3])
    for c in range(3):
        share = slabs[1, c] + arrived[0, c] + arrived[1, c]
        fresh = (fraction * fluid_vel[c] + time_step * share) / below
        window[1, c] = fresh
        fluid_out[c] = fresh
    fluid_copies = [
        remote(6, window.at[1], window.at[2], beside("gz", -1)),
        remote(7, window.at[1], window.at[0], beside("gz", 1)),
    ]
    for copy in fluid_copies:
        copy.start()

    for copy in ghost_copies:
        copy.wait()

    def build_ghost(group, carry):
        for k in range(GROUP):
            slot = pl.multiple_of((group * GROUP + k) * ROWS, ROWS)
            block = got8[pl.ds(slot, ROWS), :]
            v8[pl.ds(NT * ROWS + slot, ROWS), :] = block
            far[NT + group * GROUP + k] = far_form(block)
        return carry

    lax.fori_loop(0, NB // GROUP, build_ghost, 0)
    limits = []
    for face in range(4):
        name = names[face // 2]
        edge = 0 if face % 2 == 0 else sizes[name] - 1
        limits.append(face * GB + jnp.where(me[name] == edge, 0, ghost_counts[face]))

    def listed_too(tile):
        limit = jnp.where(tile < 2 * GB, jnp.where(tile < GB, limits[0], limits[1]),
                          jnp.where(tile < 3 * GB, limits[2], limits[3]))
        return listed(tile) + [jnp.where(tile < limit, NT + tile, DEAD)]

    sweep(0, NB, listed_too)

    for copy in fluid_copies:
        copy.wait()
    left = []
    for c in range(3):
        full = jnp.concatenate([window[0, c], window[1, c], window[2, c]], axis=0)
        high = rounded(full)
        left.append(jnp.concatenate([high, rounded(full - high)], axis=1))
    left = jnp.concatenate(left, axis=0).astype(bf16)

    def take_chunk(chunk, carry):
        hots = [onehot[chunk * step_tiles + k] for k in range(step_tiles)]
        hots = jnp.concatenate(hots, axis=1)
        spread = jnp.dot(left, jnp.concatenate([hots, hots], axis=0), preferred_element_type=f32)
        for k in range(step_tiles):
            tile = chunk * step_tiles + k
            local = cells[pl.ds(tile, 1), :] - first_cell
            mask = row_iota((HI, TILE)) == lax.shift_right_logical(local, 7)
            for c in range(3):
                part = jnp.where(mask, spread[c * HI:(c + 1) * HI, k * TILE:(k + 1) * TILE], 0.0)
                at_cell[c, pl.ds(tile, 1), :] = jnp.sum(part, axis=0, keepdims=True)
        return carry

    lax.fori_loop(0, NT // step_tiles, take_chunk, 0)

    coupling = time_step * drag_rate / masses
    per_mass = time_step / masses
    scale = 1.0 / (1.0 + coupling)
    def row_form(q):
        return sums[q].T[0:NT]

    total_weight = row_form(0)
    for c in range(3):
        speed = stiffness * (state[c] - 0.5) - damping * state[3 + c]
        force = speed * total_weight - row_form(1 + c)
        velocity_out[c] = (state[3 + c] + force * per_mass + coupling * at_cell[c]) * scale


def body(sizes, state, tile_lists, tile_counts, ghost_counts, cell_index, fluid_vel, fluid_frac):
    particles = state.shape[3]
    cell_count = fluid_vel.shape[3]
    vmem = pl.BlockSpec(memory_space=pltpu.VMEM)
    hbm = pl.BlockSpec(memory_space=pltpu.HBM)
    velocity, fluid = pl.pallas_call(
        functools.partial(kernel, sizes),
        out_shape=(
            jax.ShapeDtypeStruct((3, NT, TILE), f32),
            jax.ShapeDtypeStruct((3, ROWS, TILE), f32),
        ),
        in_specs=[hbm] * 7,
        out_specs=(vmem, vmem),
        scratch_shapes=[
            pltpu.SMEM((K, NT), jnp.int32),
            pltpu.SMEM((NT,), jnp.int32),
            pltpu.SMEM((4,), jnp.int32),
            pltpu.VMEM((7, NT, TILE), f32),
            pltpu.VMEM((NT, TILE), jnp.int32),
            pltpu.VMEM((3, ROWS, TILE), f32),
            pltpu.VMEM((ROWS, TILE), f32),
            pltpu.VMEM(((DEAD + 1) * ROWS, TILE), f32),
            pltpu.VMEM((NB * ROWS, TILE), f32),
            pltpu.VMEM((NB * ROWS, TILE), f32),
            pltpu.VMEM((NT, TILE, TILE), bf16),
            pltpu.VMEM((DEAD + 1, DEPTH, TILE), bf16),
            pltpu.VMEM((2, TILE, (K + 1) * TILE), f32),
            pltpu.VMEM((2, 4, TILE, TILE), f32),
            pltpu.VMEM((4, TILE, TILE), f32),
            pltpu.VMEM((8, NT, TILE), f32),
            pltpu.VMEM((NT, TILE, TILE), bf16),
            pltpu.VMEM((8 * HI, TILE), f32),
            pltpu.VMEM((3, 4, ROWS, TILE), f32),
            pltpu.VMEM((2, 4, ROWS, TILE), f32),
            pltpu.VMEM((3, 3, ROWS, TILE), f32),
            pltpu.VMEM((3, NT, TILE), f32),
            pltpu.SemaphoreType.DMA((8,)),
            pltpu.SemaphoreType.DMA((8,)),
            pltpu.SemaphoreType.DMA((7,)),
        ],
        compiler_params=pltpu.CompilerParams(
            collective_id=0, has_side_effects=True, vmem_limit_bytes=32 * 1024 * 1024
        ),
    )(
        *[
            pltpu.with_memory_space_constraint(value, pltpu.HBM)
            for value in (
                tile_lists.reshape(NT, K).T,
                tile_counts.reshape(NT),
                ghost_counts.reshape(4),
                state.reshape(7, NT, TILE),
                cell_index.reshape(NT, TILE),
                fluid_vel.reshape(3, ROWS, TILE),
                fluid_frac.reshape(ROWS, TILE),
            )
        ]
    )
    return velocity.reshape(3, 1, 1, particles), fluid.reshape(3, 1, 1, cell_count)


def solution(mesh):
    sizes = {name: mesh.shape[name] for name in ("gx", "gy", "gz")}
    return jax.shard_map(
        functools.partial(body, sizes),
        mesh=mesh,
        in_specs=(
            P(None, "gx", "gy", "gz"),
            P("gx", "gy", "gz", None),
            P("gx", "gy", "gz"),
            P("gx", "gy", "gz", None),
            P("gx", "gy", "gz"),
            P(None, "gx", "gy", "gz"),
            P("gx", "gy", "gz"),
        ),
        out_specs=(P(None, "gx", "gy", "gz"), P(None, "gx", "gy", "gz")),
        check_vma=False,
    )
```

```python
import functools

import jax
import jax.numpy as jnp
from jax import lax
from jax.experimental import pallas as pl
from jax.experimental.pallas import tpu as pltpu
from jax.sharding import PartitionSpec as P

TILE = 128
K = 8
NT = 64
GB = 12
NB = 4 * GB
HI = 24
ROWS = 8
DEPTH = 16
DEAD = NT + NB
GROUP = 4
UNROLL = 8

stiffness = 5.0
damping = 2.0
time_step = 0.25
drag_coef = 64.0
fluid_density = 2.0
radius_ref = 0.25
dead_level = -8192.0

f32 = jnp.float32
bf16 = jnp.bfloat16
MESH = pl.DeviceIdType.MESH


def rounded(x):
    return x.astype(bf16).astype(f32)


def pieces(x):
    high = rounded(x)
    return high, rounded(x - high)


def row_iota(shape):
    return lax.broadcasted_iota(jnp.int32, shape, 0)


def far_form(block):
    row = row_iota((ROWS, TILE))
    high, middle = pieces(block)
    first = jnp.where(row < 4, high, pltpu.roll(middle, 4, 0))
    second = jnp.where(row < 5, high, jnp.where(row == 5, pltpu.roll(middle, 1, 0), 1.0))
    return jnp.concatenate([first, second], axis=0).astype(bf16)


def near_form(block):
    row = row_iota((ROWS, TILE))
    high, middle = pieces(block)
    first = 2.0 * jnp.where(row < 4, high, pltpu.roll(high, 4, 0))
    level = jnp.where(row == 6, pltpu.roll(high, 2, 0), pltpu.roll(middle, 3, 0))
    second = jnp.where(row < 4, 2.0 * middle, jnp.where(row < 6, 1.0, level))
    return jnp.concatenate([first, second], axis=0)


def set_levels(tile, far_tiles, near, far, levels):
    heights = jnp.concatenate([far[index] for index in far_tiles], axis=1)
    width = len(far_tiles) * TILE
    rows = near[tile][:, 0:DEPTH]
    levels[:, 0:width] = jnp.dot(rows, heights, preferred_element_type=f32)


def add_far(far_tiles, v8, levels, totals):
    pulls = [[v8[pl.ds(index * ROWS + 5 + c, ROWS, stride=0), :] for c in range(3)] for index in far_tiles]
    for r in range(0, TILE, ROWS):
        held = [None] * 4
        for s, pull in enumerate(pulls):
            weight = jnp.maximum(levels[r:r + ROWS, s * TILE:(s + 1) * TILE], 0.0)
            terms = [weight] + [weight * row for row in pull]
            held = [term if total is None else total + term for total, term in zip(held, terms)]
        for q in range(4):
            totals[q, r:r + ROWS, :] = held[q]


def sum_lanes(tile, totals, sums):
    mask = lax.broadcasted_iota(jnp.int32, (ROWS, TILE), 1) == tile
    for q in range(4):
        for r in range(0, TILE, ROWS):
            column = jnp.sum(totals[q, r:r + ROWS, :], axis=1, keepdims=True)
            pltpu.store(sums.at[q, r:r + ROWS, :], jnp.broadcast_to(column, (ROWS, TILE)), mask=mask)


def kernel(
    sizes,
    lists_in, counts_in, ghost_counts_in, state_in, cells_in, fluid_vel_in, fluid_frac_in,
    base, gain, window_out,
    lists, counts, ghost_counts, state, cells, fluid_vel, fluid_frac,
    v8, send8, got8, near, far, levels, totals, sums, sources, deposit, slabs, arrived, window,
    send_sem, recv_sem, in_sem,
):
    loads = [
        pltpu.make_async_copy(source, target, in_sem.at[index])
        for index, (source, target) in enumerate([
            (state_in, state), (ghost_counts_in, ghost_counts), (cells_in, cells), (lists_in, lists),
            (counts_in, counts), (fluid_vel_in, fluid_vel), (fluid_frac_in, fluid_frac),
        ])
    ]
    for load in loads:
        load.start()
    names = ("gx", "gy", "gz")
    me = {name: lax.axis_index(name) for name in names}

    def beside(name, step):
        count = sizes[name]
        return {name: lax.rem(me[name] + step + count, count)}

    partners = [beside(name, step) for name in names for step in (-1, 1)]
    barrier = pltpu.get_barrier_semaphore()
    for partner in partners:
        pl.semaphore_signal(barrier, inc=1, device_id=partner, device_id_type=MESH)

    def remote(index, source, target, partner):
        return pltpu.make_async_remote_copy(
            src_ref=source, dst_ref=target, send_sem=send_sem.at[index], recv_sem=recv_sem.at[index],
            device_id=partner, device_id_type=MESH,
        )

    for load in loads:
        load.wait()
    radius = state[6]
    masses = radius / radius_ref
    masses = masses * masses * masses
    drag_rate = drag_coef * radius * radius
    level = radius * radius
    for c in range(3):
        centred = state[c] - 0.5
        level = level - centred * centred
        v8[pl.ds(c, NT, stride=ROWS), :] = centred
        v8[pl.ds(5 + c, NT, stride=ROWS), :] = stiffness * centred - damping * state[3 + c]
    v8[pl.ds(3, NT, stride=ROWS), :] = radius
    v8[pl.ds(4, NT, stride=ROWS), :] = level

    send8[...] = v8[pl.ds(0, NB * ROWS), :]
    row = row_iota((NB, TILE))
    limit = jnp.where(row < GB, ghost_counts[0], GB + ghost_counts[1])
    limit = jnp.where(row < 2 * GB, limit, 2 * GB + ghost_counts[2])
    limit = jnp.where(row < 3 * GB, limit, 3 * GB + ghost_counts[3])
    send8[pl.ds(4, NB, stride=ROWS), :] = jnp.where(row < limit, level[0:NB], dead_level)
    row = row_iota((ROWS, TILE))
    v8[pl.ds(DEAD * ROWS, ROWS), :] = jnp.where(row == 4, dead_level, 0.0).astype(f32)

    for c in range(3):
        high = rounded(drag_rate * state[3 + c])
        sources[c] = high
        sources[4 + c] = rounded(drag_rate * state[3 + c] - high)
    high = rounded(drag_rate)
    sources[3] = high
    sources[7] = rounded(drag_rate - high)
    first_cell = (me["gz"] - 1) * (ROWS * TILE)
    step_tiles = 16
    deposit[...] = jnp.zeros_like(deposit)

    places = row_iota((TILE, TILE)).astype(f32).astype(bf16)

    def add_chunk(chunk, carry):
        left, right = [], []
        for k in range(step_tiles):
            tile = chunk * step_tiles + k
            local = cells[pl.ds(tile, 1), :] - first_cell
            low = (local & (TILE - 1)).astype(f32).astype(bf16)
            hot = jnp.where(places == low, jnp.ones((), bf16), jnp.zeros((), bf16))
            right.append(hot)
            mask = row_iota((HI, TILE)) == lax.shift_right_logical(local, 7)
            parts = [jnp.where(mask, sources[q, pl.ds(tile, 1), :], 0.0) for q in range(8)]
            left.append(jnp.concatenate(parts, axis=0).astype(bf16))
        deposit[...] += lax.dot_general(
            jnp.concatenate(left, axis=1), jnp.concatenate(right, axis=1),
            (((1,), (1,)), ((), ())), preferred_element_type=f32,
        )
        return carry

    lax.fori_loop(0, NT // step_tiles, add_chunk, 0)
    for q in range(4):
        both = deposit[pl.ds(q * HI, HI), :] + deposit[pl.ds((4 + q) * HI, HI), :]
        for slab in range(3):
            slabs[slab, q] = both[slab * ROWS:(slab + 1) * ROWS]

    pl.semaphore_wait(barrier, len(partners))

    width = GB * ROWS
    ghost_copies = []
    for face in range(4):
        name = names[face // 2]
        step = -1 if face % 2 == 0 else 1
        opposite = face ^ 1
        ghost_copies.append(
            remote(
                face,
                send8.at[pl.ds(face * width, width), :],
                got8.at[pl.ds(opposite * width, width), :],
                beside(name, step),
            )
        )
        ghost_copies[-1].start()

    slab_copies = [
        remote(4, slabs.at[0], arrived.at[1], beside("gz", -1)),
        remote(5, slabs.at[2], arrived.at[0], beside("gz", 1)),
    ]
    for copy in slab_copies:
        copy.start()

    def block_of(tile):
        return v8[pl.ds(pl.multiple_of(tile * ROWS, ROWS), ROWS), :]

    def build_own(group, carry):
        for k in range(GROUP):
            tile = group * GROUP + k
            block = block_of(tile)
            far[tile] = far_form(block)
            near[tile, :, 0:DEPTH] = near_form(block).T.astype(bf16)
        return carry

    lax.fori_loop(0, NT // GROUP, build_own, 0)
    far[DEAD] = far_form(block_of(DEAD))
    def listed(tile):
        return [jnp.where(s < counts[tile], lists[s, tile], DEAD) for s in range(K)]

    def sweep(first, last, listing):
        set_levels(first, listing(first), near, far, levels.at[0])
        totals[1] = jnp.zeros((4, TILE, TILE), f32)

        def some_tiles(group, carry):
            for k in range(UNROLL):
                tile = first + UNROLL * group + k
                now, later = k % 2, (k + 1) % 2
                before = tile - 1 if k > 0 else jnp.where(group == 0, -1, tile - 1)
                after = tile + 1 if k < UNROLL - 1 else jnp.minimum(tile + 1, last - 1)
                add_far(listing(tile), v8, levels.at[now], totals.at[now])
                set_levels(after, listing(after), near, far, levels.at[later])
                sum_lanes(before, totals.at[later], sums)
            return carry

        lax.fori_loop(0, (last - first) // UNROLL, some_tiles, 0)
        sum_lanes(last - 1, totals.at[1], sums)

    sweep(NB, NT, listed)

    for copy in slab_copies:
        copy.wait()
    fraction = fluid_density * fluid_frac[...]
    below = fraction + time_step * (slabs[1, 3] + arrived[0, 3] + arrived[1, 3])
    for c in range(3):
        share = slabs[1, c] + arrived[0, c] + arrived[1, c]
        fresh = (fraction * fluid_vel[c] + time_step * share) / below
        window[1, c] = fresh
    fluid_copies = [
        remote(6, window.at[1], window.at[2], beside("gz", -1)),
        remote(7, window.at[1], window.at[0], beside("gz", 1)),
    ]
    for copy in fluid_copies:
        copy.start()

    for copy in ghost_copies:
        copy.wait()

    def build_ghost(group, carry):
        for k in range(GROUP):
            slot = pl.multiple_of((group * GROUP + k) * ROWS, ROWS)
            block = got8[pl.ds(slot, ROWS), :]
            v8[pl.ds(NT * ROWS + slot, ROWS), :] = block
            far[NT + group * GROUP + k] = far_form(block)
        return carry

    lax.fori_loop(0, NB // GROUP, build_ghost, 0)
    limits = []
    for face in range(4):
        name = names[face // 2]
        edge = 0 if face % 2 == 0 else sizes[name] - 1
        limits.append(face * GB + jnp.where(me[name] == edge, 0, ghost_counts[face]))

    def listed_too(tile):
        limit = jnp.where(tile < 2 * GB, jnp.where(tile < GB, limits[0], limits[1]),
                          jnp.where(tile < 3 * GB, limits[2], limits[3]))
        return listed(tile) + [jnp.where(tile < limit, NT + tile, DEAD)]

    sweep(0, NB, listed_too)

    for copy in fluid_copies:
        copy.wait()
    coupling = time_step * drag_rate / masses
    per_mass = time_step / masses
    scale = 1.0 / (1.0 + coupling)
    window_out[...] = window[...]
    gain[...] = coupling * scale
    total_weight = sums[0].T[0:NT]
    for c in range(3):
        speed = stiffness * (state[c] - 0.5) - damping * state[3 + c]
        force = speed * total_weight - sums[1 + c].T[0:NT]
        base[c] = (state[3 + c] + force * per_mass) * scale


def finish(base, gain, window, cells, velocity_out, fluid_out, at_cell):
    first_cell = (lax.axis_index("gz") - 1) * (ROWS * TILE)
    step_tiles = 16
    fluid_out[...] = window[1]
    places = row_iota((TILE, TILE)).astype(f32).astype(bf16)
    left = []
    for c in range(3):
        full = jnp.concatenate([window[0, c], window[1, c], window[2, c]], axis=0)
        high = rounded(full)
        left.append(jnp.concatenate([high, rounded(full - high)], axis=1))
    left = jnp.concatenate(left, axis=0).astype(bf16)

    def take_chunk(chunk, carry):
        hots = []
        for k in range(step_tiles):
            low = ((cells[pl.ds(chunk * step_tiles + k, 1), :] - first_cell) & (TILE - 1)).astype(f32).astype(bf16)
            hots.append(jnp.where(places == low, jnp.ones((), bf16), jnp.zeros((), bf16)))
        hots = jnp.concatenate(hots, axis=1)
        spread = jnp.dot(left, jnp.concatenate([hots, hots], axis=0), preferred_element_type=f32)
        for k in range(step_tiles):
            tile = chunk * step_tiles + k
            local = cells[pl.ds(tile, 1), :] - first_cell
            mask = row_iota((HI, TILE)) == lax.shift_right_logical(local, 7)
            for c in range(3):
                part = jnp.where(mask, spread[c * HI:(c + 1) * HI, k * TILE:(k + 1) * TILE], 0.0)
                at_cell[c, pl.ds(tile, 1), :] = jnp.sum(part, axis=0, keepdims=True)
        return carry

    lax.fori_loop(0, NT // step_tiles, take_chunk, 0)

    for c in range(3):
        velocity_out[c] = base[c] + gain[...] * at_cell[c]


def body(sizes, state, tile_lists, tile_counts, ghost_counts, cell_index, fluid_vel, fluid_frac):
    particles = state.shape[3]
    cell_count = fluid_vel.shape[3]
    vmem = pl.BlockSpec(memory_space=pltpu.VMEM)
    hbm = pl.BlockSpec(memory_space=pltpu.HBM)
    base, gain, window = pl.pallas_call(
        functools.partial(kernel, sizes),
        out_shape=(
            jax.ShapeDtypeStruct((3, NT, TILE), f32),
            jax.ShapeDtypeStruct((NT, TILE), f32),
            jax.ShapeDtypeStruct((3, 3, ROWS, TILE), f32),
        ),
        in_specs=[hbm] * 7,
        out_specs=(vmem, vmem, vmem),
        scratch_shapes=[
            pltpu.SMEM((K, NT), jnp.int32),
            pltpu.SMEM((NT,), jnp.int32),
            pltpu.SMEM((4,), jnp.int32),
            pltpu.VMEM((7, NT, TILE), f32),
            pltpu.VMEM((NT, TILE), jnp.int32),
            pltpu.VMEM((3, ROWS, TILE), f32),
            pltpu.VMEM((ROWS, TILE), f32),
            pltpu.VMEM(((DEAD + 1) * ROWS, TILE), f32),
            pltpu.VMEM((NB * ROWS, TILE), f32),
            pltpu.VMEM((NB * ROWS, TILE), f32),
            pltpu.VMEM((NT, TILE, TILE), bf16),
            pltpu.VMEM((DEAD + 1, DEPTH, TILE), bf16),
            pltpu.VMEM((2, TILE, (K + 1) * TILE), f32),
            pltpu.VMEM((2, 4, TILE, TILE), f32),
            pltpu.VMEM((4, TILE, TILE), f32),
            pltpu.VMEM((8, NT, TILE), f32),
            pltpu.VMEM((8 * HI, TILE), f32),
            pltpu.VMEM((3, 4, ROWS, TILE), f32),
            pltpu.VMEM((2, 4, ROWS, TILE), f32),
            pltpu.VMEM((3, 3, ROWS, TILE), f32),
            pltpu.SemaphoreType.DMA((8,)),
            pltpu.SemaphoreType.DMA((8,)),
            pltpu.SemaphoreType.DMA((7,)),
        ],
        compiler_params=pltpu.CompilerParams(
            collective_id=0, has_side_effects=True, vmem_limit_bytes=32 * 1024 * 1024
        ),
    )(
        *[
            pltpu.with_memory_space_constraint(value, pltpu.HBM)
            for value in (
                tile_lists.reshape(NT, K).T,
                tile_counts.reshape(NT),
                ghost_counts.reshape(4),
                state.reshape(7, NT, TILE),
                cell_index.reshape(NT, TILE),
                fluid_vel.reshape(3, ROWS, TILE),
                fluid_frac.reshape(ROWS, TILE),
            )
        ]
    )
    velocity, fluid = pl.pallas_call(
        finish,
        out_shape=(
            jax.ShapeDtypeStruct((3, NT, TILE), f32),
            jax.ShapeDtypeStruct((3, ROWS, TILE), f32),
        ),
        in_specs=[vmem] * 4,
        out_specs=(vmem, vmem),
        scratch_shapes=[pltpu.VMEM((3, NT, TILE), f32)],
        compiler_params=pltpu.CompilerParams(vmem_limit_bytes=16 * 1024 * 1024),
    )(base, gain, window, cell_index.reshape(NT, TILE))
    return velocity.reshape(3, 1, 1, particles), fluid.reshape(3, 1, 1, cell_count)


def solution(mesh):
    sizes = {name: mesh.shape[name] for name in ("gx", "gy", "gz")}
    return jax.shard_map(
        functools.partial(body, sizes),
        mesh=mesh,
        in_specs=(
            P(None, "gx", "gy", "gz"),
            P("gx", "gy", "gz", None),
            P("gx", "gy", "gz"),
            P("gx", "gy", "gz", None),
            P("gx", "gy", "gz"),
            P(None, "gx", "gy", "gz"),
            P("gx", "gy", "gz"),
        ),
        out_specs=(P(None, "gx", "gy", "gz"), P(None, "gx", "gy", "gz")),
        check_vma=False,
    )
```

```python
import functools

import jax
import jax.numpy as jnp
from jax import lax
from jax.experimental import pallas as pl
from jax.experimental.pallas import tpu as pltpu
from jax.sharding import PartitionSpec as P

TILE = 128
K = 8
NT = 64
GB = 12
NB = 4 * GB
HI = 24
ROWS = 8
DEPTH = 16
DEAD = NT + NB
GROUP = 8
UNROLL = 16

stiffness = 5.0
damping = 2.0
time_step = 0.25
drag_coef = 64.0
fluid_density = 2.0
radius_ref = 0.25
dead_level = -8192.0

f32 = jnp.float32
bf16 = jnp.bfloat16
MESH = pl.DeviceIdType.MESH


def rounded(x):
    return x.astype(bf16).astype(f32)


def pieces(x):
    high = rounded(x)
    return high, rounded(x - high)


def row_iota(shape):
    return lax.broadcasted_iota(jnp.int32, shape, 0)


def far_form(block):
    row = row_iota((ROWS, TILE))
    high, middle = pieces(block)
    first = jnp.where(row < 4, high, pltpu.roll(middle, 4, 0))
    second = jnp.where(row < 5, high, jnp.where(row == 5, pltpu.roll(middle, 1, 0), 1.0))
    return jnp.concatenate([first, second], axis=0).astype(bf16)


def near_form(block):
    row = row_iota((ROWS, TILE))
    high, middle = pieces(block)
    first = 2.0 * jnp.where(row < 4, high, pltpu.roll(high, 4, 0))
    level = jnp.where(row == 6, pltpu.roll(high, 2, 0), pltpu.roll(middle, 3, 0))
    second = jnp.where(row < 4, 2.0 * middle, jnp.where(row < 6, 1.0, level))
    return jnp.concatenate([first, second], axis=0)


def set_levels(tile, far_tiles, far, v8, levels):
    rows = near_form(v8[pl.ds(pl.multiple_of(tile * ROWS, ROWS), ROWS), :]).T.astype(bf16)
    heights = jnp.concatenate([far[index] for index in far_tiles], axis=1)
    width = len(far_tiles) * TILE
    levels[:, 0:width] = jnp.dot(rows, heights, preferred_element_type=f32)


def add_far(far_tiles, v8, levels, totals):
    pulls = [[v8[pl.ds(index * ROWS + 5 + c, ROWS, stride=0), :] for c in range(3)] for index in far_tiles]
    for r in range(0, TILE, ROWS):
        held = [None] * 4
        for s, pull in enumerate(pulls):
            weight = jnp.maximum(levels[r:r + ROWS, s * TILE:(s + 1) * TILE], 0.0)
            terms = [weight] + [weight * row for row in pull]
            held = [term if total is None else total + term for total, term in zip(held, terms)]
        for q in range(4):
            totals[q, r:r + ROWS, :] = held[q]


def sum_lanes(tile, totals, sums):
    mask = lax.broadcasted_iota(jnp.int32, (ROWS, TILE), 1) == tile
    for q in range(4):
        for r in range(0, TILE, ROWS):
            column = jnp.sum(totals[q, r:r + ROWS, :], axis=1, keepdims=True)
            pltpu.store(sums.at[q, r:r + ROWS, :], jnp.broadcast_to(column, (ROWS, TILE)), mask=mask)


def kernel(
    sizes,
    lists_in, counts_in, ghost_counts_in, state_in, cells_in, fluid_vel_in, fluid_frac_in,
    base, gain, window_out,
    lists, counts, ghost_counts, state, cells, fluid_vel, fluid_frac,
    v8, send8, got8, far, levels, totals, sums, sources, deposit, slabs, arrived, window,
    send_sem, recv_sem, in_sem,
):
    loads = [
        pltpu.make_async_copy(source, target, in_sem.at[index])
        for index, (source, target) in enumerate([
            (state_in, state), (ghost_counts_in, ghost_counts), (cells_in, cells), (lists_in, lists),
            (counts_in, counts), (fluid_vel_in, fluid_vel), (fluid_frac_in, fluid_frac),
        ])
    ]
    for load in loads:
        load.start()
    names = ("gx", "gy", "gz")
    me = {name: lax.axis_index(name) for name in names}

    def beside(name, step):
        count = sizes[name]
        return {name: lax.rem(me[name] + step + count, count)}

    partners = [beside(name, step) for name in names for step in (-1, 1)]
    barrier = pltpu.get_barrier_semaphore()
    for partner in partners:
        pl.semaphore_signal(barrier, inc=1, device_id=partner, device_id_type=MESH)

    def remote(index, source, target, partner):
        return pltpu.make_async_remote_copy(
            src_ref=source, dst_ref=target, send_sem=send_sem.at[index], recv_sem=recv_sem.at[index],
            device_id=partner, device_id_type=MESH,
        )

    for load in loads:
        load.wait()
    radius = state[6]
    masses = radius / radius_ref
    masses = masses * masses * masses
    drag_rate = drag_coef * radius * radius
    level = radius * radius
    for c in range(3):
        centred = state[c] - 0.5
        level = level - centred * centred
        v8[pl.ds(c, NT, stride=ROWS), :] = centred
        v8[pl.ds(5 + c, NT, stride=ROWS), :] = stiffness * centred - damping * state[3 + c]
    v8[pl.ds(3, NT, stride=ROWS), :] = radius
    v8[pl.ds(4, NT, stride=ROWS), :] = level

    send8[...] = v8[pl.ds(0, NB * ROWS), :]
    row = row_iota((NB, TILE))
    limit = jnp.where(row < GB, ghost_counts[0], GB + ghost_counts[1])
    limit = jnp.where(row < 2 * GB, limit, 2 * GB + ghost_counts[2])
    limit = jnp.where(row < 3 * GB, limit, 3 * GB + ghost_counts[3])
    send8[pl.ds(4, NB, stride=ROWS), :] = jnp.where(row < limit, level[0:NB], dead_level)
    row = row_iota((ROWS, TILE))
    v8[pl.ds(DEAD * ROWS, ROWS), :] = jnp.where(row == 4, dead_level, 0.0).astype(f32)

    for c in range(3):
        high = rounded(drag_rate * state[3 + c])
        sources[c] = high
        sources[4 + c] = rounded(drag_rate * state[3 + c] - high)
    high = rounded(drag_rate)
    sources[3] = high
    sources[7] = rounded(drag_rate - high)
    first_cell = (me["gz"] - 1) * (ROWS * TILE)
    step_tiles = 16
    deposit[...] = jnp.zeros_like(deposit)

    places = row_iota((TILE, TILE)).astype(f32).astype(bf16)

    def add_chunk(chunk, carry):
        left, right = [], []
        for k in range(step_tiles):
            tile = chunk * step_tiles + k
            local = cells[pl.ds(tile, 1), :] - first_cell
            low = (local & (TILE - 1)).astype(f32).astype(bf16)
            hot = jnp.where(places == low, jnp.ones((), bf16), jnp.zeros((), bf16))
            right.append(hot)
            mask = row_iota((HI, TILE)) == lax.shift_right_logical(local, 7)
            parts = [jnp.where(mask, sources[q, pl.ds(tile, 1), :], 0.0) for q in range(8)]
            left.append(jnp.concatenate(parts, axis=0).astype(bf16))
        deposit[...] += lax.dot_general(
            jnp.concatenate(left, axis=1), jnp.concatenate(right, axis=1),
            (((1,), (1,)), ((), ())), preferred_element_type=f32,
        )
        return carry

    lax.fori_loop(0, NT // step_tiles, add_chunk, 0)
    for q in range(4):
        both = deposit[pl.ds(q * HI, HI), :] + deposit[pl.ds((4 + q) * HI, HI), :]
        for slab in range(3):
            slabs[slab, q] = both[slab * ROWS:(slab + 1) * ROWS]

    pl.semaphore_wait(barrier, len(partners))

    width = GB * ROWS
    ghost_copies = []
    for face in range(4):
        name = names[face // 2]
        step = -1 if face % 2 == 0 else 1
        opposite = face ^ 1
        ghost_copies.append(
            remote(
                face,
                send8.at[pl.ds(face * width, width), :],
                got8.at[pl.ds(opposite * width, width), :],
                beside(name, step),
            )
        )
        ghost_copies[-1].start()

    slab_copies = [
        remote(4, slabs.at[0], arrived.at[1], beside("gz", -1)),
        remote(5, slabs.at[2], arrived.at[0], beside("gz", 1)),
    ]
    for copy in slab_copies:
        copy.start()

    def block_of(tile):
        return v8[pl.ds(pl.multiple_of(tile * ROWS, ROWS), ROWS), :]

    def build_own(group, carry):
        for k in range(GROUP):
            tile = group * GROUP + k
            block = block_of(tile)
            far[tile] = far_form(block)
        return carry

    lax.fori_loop(0, NT // GROUP, build_own, 0)
    far[DEAD] = far_form(block_of(DEAD))
    def listed(tile):
        return [jnp.where(s < counts[tile], lists[s, tile], DEAD) for s in range(K)]

    def sweep(first, last, listing):
        set_levels(first, listing(first), far, v8, levels.at[0])
        totals[1] = jnp.zeros((4, TILE, TILE), f32)

        def some_tiles(group, carry):
            for k in range(UNROLL):
                tile = first + UNROLL * group + k
                now, later = k % 2, (k + 1) % 2
                before = tile - 1 if k > 0 else jnp.where(group == 0, -1, tile - 1)
                after = tile + 1 if k < UNROLL - 1 else jnp.minimum(tile + 1, last - 1)
                add_far(listing(tile), v8, levels.at[now], totals.at[now])
                set_levels(after, listing(after), far, v8, levels.at[later])
                sum_lanes(before, totals.at[later], sums)
            return carry

        lax.fori_loop(0, (last - first) // UNROLL, some_tiles, 0)
        sum_lanes(last - 1, totals.at[1], sums)

    sweep(NB, NT, listed)

    for copy in slab_copies:
        copy.wait()
    fraction = fluid_density * fluid_frac[...]
    below = fraction + time_step * (slabs[1, 3] + arrived[0, 3] + arrived[1, 3])
    for c in range(3):
        share = slabs[1, c] + arrived[0, c] + arrived[1, c]
        fresh = (fraction * fluid_vel[c] + time_step * share) / below
        window[1, c] = fresh
    fluid_copies = [
        remote(6, window.at[1], window.at[2], beside("gz", -1)),
        remote(7, window.at[1], window.at[0], beside("gz", 1)),
    ]
    for copy in fluid_copies:
        copy.start()

    for copy in ghost_copies:
        copy.wait()

    def build_ghost(group, carry):
        for k in range(GROUP):
            slot = pl.multiple_of((group * GROUP + k) * ROWS, ROWS)
            block = got8[pl.ds(slot, ROWS), :]
            v8[pl.ds(NT * ROWS + slot, ROWS), :] = block
            far[NT + group * GROUP + k] = far_form(block)
        return carry

    lax.fori_loop(0, NB // GROUP, build_ghost, 0)
    limits = []
    for face in range(4):
        name = names[face // 2]
        edge = 0 if face % 2 == 0 else sizes[name] - 1
        limits.append(face * GB + jnp.where(me[name] == edge, 0, ghost_counts[face]))

    def listed_too(tile):
        limit = jnp.where(tile < 2 * GB, jnp.where(tile < GB, limits[0], limits[1]),
                          jnp.where(tile < 3 * GB, limits[2], limits[3]))
        return listed(tile) + [jnp.where(tile < limit, NT + tile, DEAD)]

    sweep(0, NB, listed_too)

    for copy in fluid_copies:
        copy.wait()
    coupling = time_step * drag_rate / masses
    per_mass = time_step / masses
    scale = 1.0 / (1.0 + coupling)
    window_out[...] = window[...]
    gain[...] = coupling * scale
    total_weight = sums[0].T[0:NT]
    for c in range(3):
        speed = stiffness * (state[c] - 0.5) - damping * state[3 + c]
        force = speed * total_weight - sums[1 + c].T[0:NT]
        base[c] = (state[3 + c] + force * per_mass) * scale


def finish(base, gain, window, cells, velocity_out, fluid_out, at_cell):
    first_cell = (lax.axis_index("gz") - 1) * (ROWS * TILE)
    step_tiles = 16
    fluid_out[...] = window[1]
    places = row_iota((TILE, TILE)).astype(f32).astype(bf16)
    left = []
    for c in range(3):
        full = jnp.concatenate([window[0, c], window[1, c], window[2, c]], axis=0)
        high = rounded(full)
        left.append(jnp.concatenate([high, rounded(full - high)], axis=1))
    left = jnp.concatenate(left, axis=0).astype(bf16)

    def take_chunk(chunk, carry):
        hots = []
        for k in range(step_tiles):
            low = ((cells[pl.ds(chunk * step_tiles + k, 1), :] - first_cell) & (TILE - 1)).astype(f32).astype(bf16)
            hots.append(jnp.where(places == low, jnp.ones((), bf16), jnp.zeros((), bf16)))
        hots = jnp.concatenate(hots, axis=1)
        spread = jnp.dot(left, jnp.concatenate([hots, hots], axis=0), preferred_element_type=f32)
        for k in range(step_tiles):
            tile = chunk * step_tiles + k
            local = cells[pl.ds(tile, 1), :] - first_cell
            mask = row_iota((HI, TILE)) == lax.shift_right_logical(local, 7)
            for c in range(3):
                part = jnp.where(mask, spread[c * HI:(c + 1) * HI, k * TILE:(k + 1) * TILE], 0.0)
                at_cell[c, pl.ds(tile, 1), :] = jnp.sum(part, axis=0, keepdims=True)
        return carry

    lax.fori_loop(0, NT // step_tiles, take_chunk, 0)

    for c in range(3):
        velocity_out[c] = base[c] + gain[...] * at_cell[c]


def body(sizes, state, tile_lists, tile_counts, ghost_counts, cell_index, fluid_vel, fluid_frac):
    particles = state.shape[3]
    cell_count = fluid_vel.shape[3]
    vmem = pl.BlockSpec(memory_space=pltpu.VMEM)
    hbm = pl.BlockSpec(memory_space=pltpu.HBM)
    base, gain, window = pl.pallas_call(
        functools.partial(kernel, sizes),
        out_shape=(
            jax.ShapeDtypeStruct((3, NT, TILE), f32),
            jax.ShapeDtypeStruct((NT, TILE), f32),
            jax.ShapeDtypeStruct((3, 3, ROWS, TILE), f32),
        ),
        in_specs=[hbm] * 7,
        out_specs=(vmem, vmem, vmem),
        scratch_shapes=[
            pltpu.SMEM((K, NT), jnp.int32),
            pltpu.SMEM((NT,), jnp.int32),
            pltpu.SMEM((4,), jnp.int32),
            pltpu.VMEM((7, NT, TILE), f32),
            pltpu.VMEM((NT, TILE), jnp.int32),
            pltpu.VMEM((3, ROWS, TILE), f32),
            pltpu.VMEM((ROWS, TILE), f32),
            pltpu.VMEM(((DEAD + 1) * ROWS, TILE), f32),
            pltpu.VMEM((NB * ROWS, TILE), f32),
            pltpu.VMEM((NB * ROWS, TILE), f32),
            pltpu.VMEM((DEAD + 1, DEPTH, TILE), bf16),
            pltpu.VMEM((2, TILE, (K + 1) * TILE), f32),
            pltpu.VMEM((2, 4, TILE, TILE), f32),
            pltpu.VMEM((4, TILE, TILE), f32),
            pltpu.VMEM((8, NT, TILE), f32),
            pltpu.VMEM((8 * HI, TILE), f32),
            pltpu.VMEM((3, 4, ROWS, TILE), f32),
            pltpu.VMEM((2, 4, ROWS, TILE), f32),
            pltpu.VMEM((3, 3, ROWS, TILE), f32),
            pltpu.SemaphoreType.DMA((8,)),
            pltpu.SemaphoreType.DMA((8,)),
            pltpu.SemaphoreType.DMA((7,)),
        ],
        compiler_params=pltpu.CompilerParams(
            collective_id=0, has_side_effects=True, vmem_limit_bytes=32 * 1024 * 1024
        ),
    )(
        *[
            pltpu.with_memory_space_constraint(value, pltpu.HBM)
            for value in (
                tile_lists.reshape(NT, K).T,
                tile_counts.reshape(NT),
                ghost_counts.reshape(4),
                state.reshape(7, NT, TILE),
                cell_index.reshape(NT, TILE),
                fluid_vel.reshape(3, ROWS, TILE),
                fluid_frac.reshape(ROWS, TILE),
            )
        ]
    )
    velocity, fluid = pl.pallas_call(
        finish,
        out_shape=(
            jax.ShapeDtypeStruct((3, NT, TILE), f32),
            jax.ShapeDtypeStruct((3, ROWS, TILE), f32),
        ),
        in_specs=[vmem] * 4,
        out_specs=(vmem, vmem),
        scratch_shapes=[pltpu.VMEM((3, NT, TILE), f32)],
        compiler_params=pltpu.CompilerParams(vmem_limit_bytes=16 * 1024 * 1024),
    )(base, gain, window, cell_index.reshape(NT, TILE))
    return velocity.reshape(3, 1, 1, particles), fluid.reshape(3, 1, 1, cell_count)


def solution(mesh):
    sizes = {name: mesh.shape[name] for name in ("gx", "gy", "gz")}
    return jax.shard_map(
        functools.partial(body, sizes),
        mesh=mesh,
        in_specs=(
            P(None, "gx", "gy", "gz"),
            P("gx", "gy", "gz", None),
            P("gx", "gy", "gz"),
            P("gx", "gy", "gz", None),
            P("gx", "gy", "gz"),
            P(None, "gx", "gy", "gz"),
            P("gx", "gy", "gz"),
        ),
        out_specs=(P(None, "gx", "gy", "gz"), P(None, "gx", "gy", "gz")),
        check_vma=False,
    )
```
